32 devices in a mesh: group: 2 (over x), ctx: 8 (over z, y), tp: 2 (over core).
Axes of the slice: x: 2, y: 2, z: 4, core: 2. Of those that a mesh axis runs over, the one named last changes fastest.
Arguments:
- x_in: bfloat16 [4096, 4096], P(('group', 'ctx', 'tp')), parts along dimension 0, may hold values from -6 to 6
- b_in: bfloat16 [4096, 512], P(('group', 'ctx', 'tp')), parts along dimension 0, may hold values from -6 to 6
- c_in: bfloat16 [4096, 512], P(('group', 'ctx', 'tp')), parts along dimension 0, may hold values from -6 to 6
- z_in: bfloat16 [4096, 4096], P(('group', 'ctx', 'tp')), parts along dimension 0, may hold values from -6 to 6
- dt_raw: bfloat16 [4096, 64], P(('group', 'ctx', 'tp')), parts along dimension 0, may hold values from -3 to 3
- conv_x: float32 [4, 4096], replicated, may hold values from -3 to 3
- conv_b: float32 [4, 512], replicated, may hold values from -3 to 3
- conv_c: float32 [4, 512], replicated, may hold values from -3 to 3
- decay_rate: float32 [64], replicated, may hold values from 3e-05 to 0.06
- dt_bias: float32 [64], replicated, may hold values from -1.5 to -0.5
- skip_scale: float32 [64], replicated, may hold values from 0.5 to 1.5
- norm_gain: float32 [4096], replicated, may hold values from 0.1 to 1.9
- w_value: float32 [4096], replicated, may hold values from -0.4 to 0.4
- resets: int32 [4096], P(('group', 'ctx')), parts along dimension 0, may hold values 0 or 1
- bucket: int32 [4096], P(('group', 'ctx')), parts along dimension 0, may hold values from 0 to 255
- return_table: float32 [256], replicated, may hold values from -16 to 16
Outputs:
- values: float32 [4096], P(('group', 'ctx', 'tp')), parts along dimension 0
- grad_x: bfloat16 [4096, 4096], P(('group', 'ctx', 'tp')), parts along dimension 0
- grad_b: bfloat16 [4096, 512], P(('group', 'ctx', 'tp')), parts along dimension 0
- grad_c: bfloat16 [4096, 512], P(('group', 'ctx', 'tp')), parts along dimension 0
- grad_z: bfloat16 [4096, 4096], P(('group', 'ctx', 'tp')), parts along dimension 0
- grad_dt: bfloat16 [4096, 64], P(('group', 'ctx', 'tp')), parts along dimension 0
The draws below stay inside these ranges and needn't reach their ends.
There are 2 independent parts, one for each index of `group`. The reference program is written for one: setup_inputs(seed, part) draws one part's arguments, and reference() takes and returns one part's arrays. A program takes and returns all parts, laid end to end along the dimension named above; an argument that names none is the same for every part. Nothing has to cross between parts.
All inputs are finite; a program needn't handle non-finite values. No bound on the sum of `resets` on one device may be relied on, other than what follows from the above.
Results may differ from the reference program's by a relative error of at most 0.0058.
Values may be sent and summed in bfloat16 or wider, within the bound.
A program may use at most 192 MiB of HBM per device.

```python
import math
from functools import partial
import jax
import jax.numpy as jnp
from jax import lax

HEADS = 64
HEAD_DIM = 64
STATE = 128
GROUPS = 4
BLOCK = 128
BUCKETS = 256
SEQ = 2048
CH = 4096


def set_ends(result, rng, low, top_value):
    longest = result.shape.index(max(result.shape))
    spots = []
    for shift in (0, 1):
        where = [jax.random.randint(jax.random.fold_in(rng, axis), (), 0, length) for axis, length in enumerate(result.shape)]
        where[longest] = (where[longest] + shift) % result.shape[longest]
        spots.append(tuple(where))
    return result.at[spots[0]].set(low).at[spots[1]].set(top_value)


def block_levels(key, shape, cuts, low, top_value):
    def one(dim, parts):
        draws = jax.random.uniform(jax.random.fold_in(jax.random.fold_in(key, 6), dim), (parts,), jnp.float32, low / len(cuts), top_value / len(cuts))
        return jnp.repeat(jnp.exp(draws), shape[dim] // parts).reshape((-1,) + (1,) * (len(shape) - dim - 1))

    loudness = one(*cuts[0])
    for cut in cuts[1:]:
        loudness = loudness * one(*cut)
    return loudness


def centred(stream_key, extent, deviation, limit, split=(), kind=jnp.bfloat16):
    values = jax.random.normal(stream_key, extent, jnp.float32) * deviation
    if len(split) > 0:
        values = block_levels(stream_key, extent, split, -0.22, 0.18) * values
    return jnp.clip(values, min=-limit, max=limit).astype(kind)


def setup_inputs(seed: int = 0, part: int = 0) -> dict:
    key_list = jax.random.split(jax.random.key(seed), 17)
    part_keys = jax.random.split(jax.random.fold_in(key_list[16], part), 17)
    x_in = centred(part_keys[0], (SEQ, CH), 1.0, 6.0, ((0, 16),))
    b_in = centred(part_keys[1], (SEQ, GROUPS * STATE), 1.0, 6.0, ((0, 16),))
    c_in = centred(part_keys[2], (SEQ, GROUPS * STATE), 1.0, 6.0, ((0, 16),))
    z_in = centred(part_keys[3], (SEQ, CH), 1.0, 6.0, ((0, 16),))
    dt_raw = centred(part_keys[4], (SEQ, HEADS), 0.6, 3.0, ((0, 16),))
    conv_x = centred(key_list[5], (4, CH), 0.5, 3.0, (), jnp.float32)
    conv_b = centred(key_list[6], (4, GROUPS * STATE), 0.5, 3.0, (), jnp.float32)
    conv_c = centred(key_list[7], (4, GROUPS * STATE), 0.5, 3.0, (), jnp.float32)
    decay_rate = jnp.clip(jnp.exp(jax.random.uniform(key_list[8], (HEADS,), jnp.float32, math.log(2.9999999242136255e-05), math.log(0.06))), 2.9999999242136255e-05, 0.06)
    dt_bias = jnp.clip(jax.random.uniform(key_list[9], (HEADS,), jnp.float32, -1.5, -0.5), -1.5, -0.5)
    skip_scale = jnp.clip(jax.random.uniform(key_list[10], (HEADS,), jnp.float32, 0.5, 1.5), 0.5, 1.5)
    norm_gain = jnp.clip(1.0 + 0.18 * jax.random.normal(key_list[11], (CH,), jnp.float32), 0.1, 1.9)
    w_value = centred(key_list[12], (CH,), 0.0625, 0.4, (), jnp.float32)
    resets = set_ends((jax.random.randint(part_keys[13], (SEQ,), 0, 2048) < 1).astype(jnp.int32), jax.random.fold_in(part_keys[13], 1), 0, 1)
    bucket = set_ends(jax.random.randint(part_keys[14], (SEQ,), 0, BUCKETS), jax.random.fold_in(part_keys[14], 1), 0, BUCKETS - 1).astype(jnp.int32)
    return_table = centred(key_list[15], (BUCKETS,), 4.0, 16.0, (), jnp.float32)
    return dict(x_in=x_in, b_in=b_in, c_in=c_in, z_in=z_in, dt_raw=dt_raw, conv_x=conv_x, conv_b=conv_b, conv_c=conv_c, decay_rate=decay_rate, dt_bias=dt_bias, skip_scale=skip_scale, norm_gain=norm_gain, w_value=w_value, resets=resets, bucket=bucket, return_table=return_table)


epsilon = 1e-05
highest = lax.Precision.HIGHEST

def round_keep(value):
    narrow = lax.optimization_barrier(value.astype(jnp.bfloat16))
    return value + lax.stop_gradient(narrow.astype(jnp.float32) - value)

def shift_rows(values, amount):
    filler = jnp.zeros((amount,) + values.shape[1:], values.dtype)
    return jnp.concatenate([filler, values[:values.shape[0] - amount]], axis=0)

def seen_resets(reset_real):
    first = reset_real
    second = jnp.maximum(first, shift_rows(reset_real, 1))
    third = jnp.maximum(second, shift_rows(reset_real, 2))
    return (first, second, third)

def conv_silu(extended, weight, seen_flags):
    row_count = extended.shape[0] - 3
    summed = weight[0][None, :] * extended[3:]
    for offset in range(1, 4):
        valid = 1.0 - seen_flags[offset - 1]
        summed = summed + weight[offset][None, :] * extended[3 - offset:3 - offset + row_count] * valid[:, None]
    return round_keep(jax.nn.silu(summed))

def block_decays(dt_rows, decay_rate, reset_real):
    cumulative = jnp.cumsum(-dt_rows * decay_rate[None, :], axis=0)
    counts = jnp.cumsum(reset_real, axis=0)
    return (cumulative, counts)

def block_state(x_conv, b_conv, dt_rows, cumulative, counts, per_group):
    row_count, head_count = dt_rows.shape
    alive = jnp.where(counts == counts[-1], 1.0, 0.0)
    weight_end = jnp.exp(cumulative[-1][None, :] - cumulative) * alive[:, None] * dt_rows
    x_heads = x_conv.reshape(row_count, head_count, -1) * weight_end[:, :, None]
    b_heads = jnp.repeat(b_conv.reshape(row_count, head_count // per_group, -1), per_group, axis=1)
    state_add = jnp.einsum('shp,shn->hpn', x_heads, b_heads, precision=highest)
    block_decay = jnp.exp(cumulative[-1]) * jnp.where(counts[-1] == 0.0, 1.0, 0.0)
    return (state_add, block_decay)

def block_output(x_conv, b_conv, c_conv, dt_rows, cumulative, counts, start_state, per_group):
    row_count, head_count = dt_rows.shape
    group_count = head_count // per_group
    b_groups = b_conv.reshape(row_count, group_count, -1)
    c_groups = c_conv.reshape(row_count, group_count, -1)
    scores = jnp.einsum('tgn,sgn->gts', c_groups, b_groups, precision=highest)
    rows_iota = lax.broadcasted_iota(jnp.int32, (row_count, row_count), 0)
    cols_iota = lax.broadcasted_iota(jnp.int32, (row_count, row_count), 1)
    same_seg = (rows_iota >= cols_iota) & (counts[:, None] == counts[None, :])
    log_gap = cumulative.T[:, :, None] - cumulative.T[:, None, :]
    fading = jnp.where(same_seg[None], jnp.exp(jnp.minimum(log_gap, 0.0)), 0.0)
    mixing = jnp.repeat(scores, per_group, axis=0) * fading * dt_rows.T[:, None, :]
    within = jnp.einsum('hts,shp->thp', mixing, x_conv.reshape(row_count, head_count, -1), precision=highest)
    c_heads = jnp.repeat(c_groups, per_group, axis=1)
    carried = jnp.einsum('thn,hpn->thp', c_heads, start_state, precision=highest)
    reach_decay = jnp.exp(cumulative) * jnp.where(counts == 0.0, 1.0, 0.0)[:, None]
    return (within + carried * reach_decay[:, :, None]).reshape(row_count, -1)

def reference(x_in, b_in, c_in, z_in, dt_raw, conv_x, conv_b, conv_c, decay_rate, dt_bias, skip_scale, norm_gain, w_value, resets, bucket, return_table):
    per_group = HEADS // GROUPS
    reset_real = resets.astype(jnp.float32)
    seen_flags = seen_resets(reset_real)
    block_total = SEQ // BLOCK
    emit = jax.checkpoint(partial(block_output, per_group=per_group))

    def split_blocks(array):
        return array.reshape((block_total, BLOCK) + array.shape[1:])

    def padded(array):
        return jnp.concatenate([jnp.zeros((3, array.shape[1]), jnp.float32), array], axis=0)

    def forward(x_real, b_real, c_real, z_real, dt_real):
        x_conv = conv_silu(padded(x_real), conv_x, seen_flags)
        b_conv = conv_silu(padded(b_real), conv_b, seen_flags)
        c_conv = conv_silu(padded(c_real), conv_c, seen_flags)
        dt_rows = jax.nn.softplus(dt_real + dt_bias[None, :])

        def advance(state_now, pieces):
            x_piece, b_piece, c_piece, dt_piece, reset_piece = pieces
            cumulative, counts = block_decays(dt_piece, decay_rate, reset_piece)
            output = emit(x_piece, b_piece, c_piece, dt_piece, cumulative, counts, state_now)
            state_add, block_decay = block_state(x_piece, b_piece, dt_piece, cumulative, counts, per_group)
            return (block_decay[:, None, None] * state_now + state_add, output)
        initial = jnp.zeros((HEADS, HEAD_DIM, STATE), jnp.float32)
        pieces = (split_blocks(x_conv), split_blocks(b_conv), split_blocks(c_conv), split_blocks(dt_rows), split_blocks(reset_real))
        _, outputs = lax.scan(advance, initial, pieces)
        mixed = outputs.reshape(SEQ, HEADS, HEAD_DIM) + skip_scale[None, :, None] * x_conv.reshape(SEQ, HEADS, HEAD_DIM)
        gated = mixed.reshape(SEQ, -1) * jax.nn.silu(z_real)
        norm_rms = jnp.sqrt(lax.optimization_barrier(jnp.sum(gated * gated, axis=1)) / (HEADS * HEAD_DIM) + epsilon)
        return lax.optimization_barrier(jnp.sum(gated * (norm_gain * w_value)[None, :], axis=1)) / norm_rms
    values, pull_back = jax.vjp(forward, x_in.astype(jnp.float32), b_in.astype(jnp.float32), c_in.astype(jnp.float32), z_in.astype(jnp.float32), dt_raw.astype(jnp.float32))
    value_grad = values - return_table[bucket]
    grad_x, grad_b, grad_c, grad_z, grad_dt = pull_back(value_grad)
    return (values, grad_x.astype(jnp.bfloat16), grad_b.astype(jnp.bfloat16), grad_c.astype(jnp.bfloat16), grad_z.astype(jnp.bfloat16), grad_dt.astype(jnp.bfloat16))
```

```python
from functools import partial

import jax
import jax.numpy as jnp
from jax import lax
from jax.experimental import pallas as pl
from jax.experimental.pallas import tpu as pltpu
from jax.sharding import PartitionSpec as P

HEAD_DIM = 64
STATE = 128
LANES = 128
WIDE = 256
MESH = pl.DeviceIdType.MESH

epsilon = 1e-05
f32 = jnp.float32
bf16 = jnp.bfloat16


def dot(a, b, ca=1, cb=0):
    return lax.dot_general(a, b, (((ca,), (cb,)), ((), ())), preferred_element_type=f32)


def sigmoid(u):
    return 1.0 / (1.0 + jnp.exp(-u))


def iota(shape, dim):
    return lax.broadcasted_iota(jnp.int32, shape, dim)


def two(v):
    high = v.astype(bf16)
    return high, (v - high.astype(f32)).astype(bf16)


def three(v):
    high = v.astype(bf16)
    rest = v - high.astype(f32)
    middle = rest.astype(bf16)
    return high, middle, (rest - middle.astype(f32)).astype(bf16)


def exact_dot(select, v):
    return sum(dot(select, part) for part in three(v))


def twice(v):
    return jnp.concatenate([v, v], axis=1)


INPUTS = (
    "x_in", "b_in", "c_in", "z_in", "dt_in", "conv_x", "conv_b", "conv_c", "head_rows",
    "chan_rows", "resets", "bucket", "table",
)
OUTPUTS = (
    "o_values", "o_gx", "o_gb", "o_gc", "o_gz", "o_gdt",
)


def scratch_table(T, W, N, H, tn):
    G, C = N // STATE, W // WIDE
    K = C // 2
    per = K // G
    V, D, R = pltpu.VMEM, pltpu.SemaphoreType.DMA, pltpu.SemaphoreType.REGULAR
    return dict(
        x=V((T, W), bf16), b=V((T, N), bf16), c=V((T, N), bf16), z=V((T, W), bf16),
        dt_raw=V((T, H), bf16), wx=V((4, W), f32), wb=V((4, N), f32), wc=V((4, N), f32),
        heads=V((3, H), f32), chans=V((2, W), f32), rs=V((2, T), jnp.int32),
        bk=V((2, T), jnp.int32), tab=V((1, tn), f32),
        vals=V((1, T), f32), gx=V((T, W), bf16), gb=V((T, N), bf16), gc=V((T, N), bf16),
        gz=V((T, W), bf16), gdt=V((T, H), bf16),
        halo_out=V((16, (W + 2 * N) // 2), bf16), halo_in=V((16, (W + 2 * N) // 2), bf16),
        tail=V((8, W + 2 * N), f32),
        edge_out=V((K, 8, 6 * LANES), f32), edge_in=V((K, 8, 6 * LANES), f32),
        last=V((K, 16, 6 * LANES), f32),
        dec_out=V((8, LANES), f32), dec_in=V((3, 8, LANES), f32),
        valid=V((3, T, LANES), f32), shifted=V((3, T + 8, LANES), f32),
        mask=V((T, T), f32), start_alive=V((T, LANES), f32), end_alive=V((T, LANES), f32),
        keep=V((16, LANES), f32), target=V((T, LANES), f32),
        pos=V((T + 8, LANES), f32),
        dt=V((T, H), f32), dtp=V((T, H), f32),
        ehl=V((T, 2 * H), bf16), whl=V((T, 2 * H), bf16),
        sel=V((C, 2 * H, WIDE), bf16), rows=V((C, 8, WIDE), f32),
        peer_rows=V((C, 8, WIDE), f32), gw=V((1, W), f32),
        ext=V((2, T + 8, LANES), f32), back=V((2, T + 16, LANES), f32),
        us=V((C, T, WIDE), f32), xc=V((C, T, WIDE), bf16), xs=V((C, 2 * T, WIDE), bf16),
        qg=V((C, 2 * T, WIDE), bf16), yr=V((C, T, WIDE), f32), dy=V((C, T, WIDE), f32),
        ub=V((G, T, STATE), f32), uc=V((G, T, STATE), f32),
        bc=V((G, T, STATE), bf16), cc=V((G, T, STATE), bf16),
        gcr=V((G, T, 2 * T), bf16), gtb=V((G, T, 2 * T), bf16),
        bat=V((G, STATE, T), bf16), crt=V((G, STATE, T), bf16),
        dbs=V((G, T, STATE), f32), dbacc=V((T, STATE), f32),
        sq=V((T, LANES), f32), nu=V((T, LANES), f32),
        vs=V((T, LANES), f32), co=V((T, LANES), f32),
        h1=V((T, 2 * H), f32), h2=V((T, 2 * H), f32), ends=V((C, 8, WIDE), f32),
        add=V((2, C, STATE, WIDE), bf16), sib_add=V((2, K, STATE, WIDE), bf16),
        chip_add=V((2, K, STATE, WIDE), bf16), peer_add=V((2, K, STATE, WIDE), bf16),
        going=V((2, K, STATE, WIDE), bf16), came=V((2, K, STATE, WIDE), bf16),
        sib_start=V((2, K, STATE, WIDE), bf16),
        in_sem=D((13,)), out_sem=D((K + 6,)), halo_sem=D((2,)), dec_sem=D((2, 3)),
        edge_sem=D((2, K)), sem=D((2, 4, 2, K)),
    )


def kernel(cn, tn, dims, names, *refs):
    r = dict(zip(list(INPUTS) + list(OUTPUTS) + list(names), refs))

    class Bag:
        pass

    s = Bag()
    for key, ref in r.items():
        setattr(s, key, ref)
    T, W, N, H = dims
    G, C = N // STATE, W // WIDE
    K = C // 2
    per = K // G

    ctx, tp = lax.axis_index("ctx"), lax.axis_index("tp")
    side = lax.rem(ctx, 2)
    peer = ctx + 1 - 2 * side
    sib = {"tp": 1 - tp}
    ypeer = {"ctx": peer}
    yother = {"ctx": peer, "tp": 1 - tp}
    level, levels = lax.div(ctx, 2), cn // 2
    lower_level, upper_level = level > 0, level < levels - 1
    next_block = {"ctx": ctx + tp, "tp": 1 - tp}
    prev_block = {"ctx": ctx - 1 + tp, "tp": 1 - tp}
    has_next = jnp.logical_or(tp == 0, ctx < cn - 1)
    has_prev = jnp.logical_or(tp == 1, ctx > 0)
    cross_next = jnp.logical_and(tp == 1, ctx < cn - 1)
    cross_prev = jnp.logical_and(tp == 0, ctx > 0)

    loads = [
        pltpu.make_async_copy(src, dst, s.in_sem.at[i])
        for i, (src, dst) in enumerate([
            (s.resets, s.rs), (s.x_in, s.x), (s.b_in, s.b), (s.c_in, s.c),
            (s.dt_in, s.dt_raw), (s.head_rows, s.heads), (s.bucket, s.bk), (s.table, s.tab),
            (s.conv_x, s.wx), (s.conv_b, s.wb), (s.conv_c, s.wc), (s.chan_rows, s.chans),
            (s.z_in, s.z),
        ])
    ]
    for load in loads:
        load.start()

    barrier = pltpu.get_barrier_semaphore()

    def greet(device):
        pl.semaphore_signal(barrier, inc=1, device_id=device, device_id_type=MESH)

    greet(sib)
    greet(ypeer)
    greet(yother)
    pl.when(upper_level)(lambda: greet({"ctx": ctx + 2}))
    pl.when(lower_level)(lambda: greet({"ctx": ctx - 2}))
    pl.when(cross_next)(lambda: greet(next_block))
    pl.when(cross_prev)(lambda: greet(prev_block))

    def one(flag):
        return jnp.where(flag, 1, 0)

    row_i, col_i = iota((T, T), 0), iota((T, T), 1)
    eye = row_i == col_i
    lower = row_i >= col_i

    def column(row):
        return jnp.sum(jnp.where(eye, row, 0.0), axis=1, keepdims=True)

    loads[0].wait()
    real = jnp.broadcast_to(column(s.rs[pl.ds(tp, 1), :].astype(f32)), (T, LANES))
    s.pos[0:8, :] = jnp.zeros((8, LANES), f32)
    s.pos[8 : 8 + T, :] = real
    last_r = s.pos[T + 7 : T + 8, :]
    last_two = jnp.maximum(last_r, s.pos[T + 6 : T + 7, :])
    at = iota((16, LANES), 0)
    keep = jnp.where(at == 13, 1.0 - last_two, jnp.where(at == 14, 1.0 - last_r, 1.0))
    s.keep[...] = keep
    keep8 = keep[8:16, 0:1]

    for i in (1, 2, 3):
        loads[i].wait()
    ends = [ref[T - 16 : T, :].astype(f32)[8:16] * keep8 for ref in (s.x, s.b, s.c)]
    ends = jnp.concatenate(ends, axis=1)
    half = (W + 2 * N) // 2
    s.halo_out[...] = jnp.concatenate([ends[:, :half], ends[:, half:]], axis=0).astype(bf16)
    pl.semaphore_wait(
        barrier, 3 + one(upper_level) + one(lower_level) + one(cross_next) + one(cross_prev)
    )
    halo = pltpu.make_async_remote_copy(
        src_ref=s.halo_out, dst_ref=s.halo_in, send_sem=s.halo_sem.at[0],
        recv_sem=s.halo_sem.at[1], device_id=next_block, device_id_type=MESH,
    )
    pl.when(has_next)(lambda: halo.start())

    loads[4].wait()
    loads[5].wait()
    rate, bias, skip = s.heads[0:1, :], s.heads[1:2, :], s.heads[2:3, :]
    dtp = s.dt_raw[...].astype(f32) + bias
    dt = jnp.maximum(dtp, 0.0) + jnp.log1p(jnp.exp(-jnp.abs(dtp)))
    s.dtp[...] = dtp
    s.dt[...] = dt
    low = jnp.where(lower, 1.0, 0.0).astype(bf16)
    cum = exact_dot(low, -dt * rate)
    counts = dot(low, real.astype(bf16))
    total = counts[T - 1 : T, :]
    cum_end = cum[T - 1 : T, :]
    eend = jnp.exp(cum_end)
    decay = eend * jnp.where(total[:, :H] == 0.0, 1.0, 0.0)
    s.dec_out[...] = jnp.broadcast_to(twice(decay), (8, 2 * H))

    def tell(i, device):
        return pltpu.make_async_remote_copy(
            src_ref=s.dec_out, dst_ref=s.dec_in.at[i], send_sem=s.dec_sem.at[0, i],
            recv_sem=s.dec_sem.at[1, i], device_id=device, device_id_type=MESH,
        )

    tells = [tell(0, sib), tell(1, ypeer), tell(2, yother)]
    for t in tells:
        t.start()

    s.mask[...] = jnp.where(jnp.logical_and(lower, counts == counts.T), 1.0, 0.0)
    s.start_alive[...] = jnp.where(counts == 0.0, 1.0, 0.0)
    s.end_alive[...] = jnp.where(counts == total, 1.0, 0.0)
    one_back, two_back = s.pos[7 : 7 + T, :], s.pos[6 : 6 + T, :]
    second = jnp.maximum(real, one_back)
    for k, flag in enumerate([real, second, jnp.maximum(second, two_back)]):
        s.valid[k] = 1.0 - flag
    for k in range(3):
        m = k + 1
        s.shifted[k, 0:8, :] = jnp.zeros((8, LANES), f32)
        s.shifted[k, T : T + 8, :] = jnp.zeros((8, LANES), f32)
        s.shifted[k, 8 - m : 8 - m + T, :] = s.valid[k]
    for i in range(2):
        s.back[i, 0:8, :] = jnp.zeros((8, LANES), f32)
        s.back[i, T + 8 : T + 16, :] = jnp.zeros((8, LANES), f32)
    s.ehl[...] = jnp.concatenate(two(jnp.exp(cum)), axis=1)
    s.whl[...] = jnp.concatenate(two(jnp.exp(-cum) * dt), axis=1)

    head = lax.rem(iota((2 * H, WIDE), 0), H)
    lane_head = lax.div(iota((2 * H, WIDE), 1), HEAD_DIM)

    small = jnp.concatenate([eend, decay, skip] + [jnp.zeros((1, H), f32)] * 5, axis=0)
    small = jnp.concatenate(two(small), axis=1)

    def make_sel(j, carry):
        sel = jnp.where(head == lane_head + j * (WIDE // HEAD_DIM), 1.0, 0.0).astype(bf16)
        s.sel[j] = sel
        s.rows[j] = dot(small, sel)
        return carry

    lax.fori_loop(0, C, make_sel, 0)

    for i in range(6, 12):
        loads[i].wait()
    s.gw[...] = s.chans[0:1, :] * s.chans[1:2, :]
    place = column(s.bk[pl.ds(tp, 1), :].astype(f32))
    tabled = jnp.where(place == iota((T, tn), 1).astype(f32), s.tab[...], 0.0)
    s.target[...] = jnp.broadcast_to(jnp.sum(tabled, axis=1, keepdims=True), (T, LANES))

    @pl.when(has_prev)
    def _():
        halo.wait_recv()

    @pl.when(jnp.logical_not(has_prev))
    def _():
        s.halo_in[...] = jnp.zeros(s.halo_in.shape, bf16)

    got = s.halo_in[...].astype(f32)
    s.tail[...] = jnp.concatenate([got[0:8], got[8:16]], axis=1)

    def conv_pre(slot, piece, tail, w):
        ext = s.ext.at[slot]
        ext[0:8, :] = tail
        ext[8 : 8 + T, :] = piece
        u = w[0:1] * piece
        for k in range(1, 4):
            u = u + (w[k : k + 1] * ext[8 - k : 8 - k + T, :]) * s.valid[k - 1]
        return u

    def conv_back(slot, du, w):
        ext = s.back.at[slot]
        ext[8 : 8 + T, :] = du
        g = w[0:1] * ext[0 : T + 8, :]
        for k in range(1, 4):
            g = g + (w[k : k + 1] * ext[k : k + T + 8, :]) * s.shifted[k - 1]
        return g[0:8], g[8:]

    def silu_back(g, u):
        sg = sigmoid(u)
        return g * (sg * (1.0 + u * (1.0 - sg)))

    def lanes(j, i):
        return pl.ds(pl.multiple_of(j * WIDE + i * LANES, LANES), LANES)

    def cols(i):
        return slice(i * LANES, (i + 1) * LANES)

    def ship(way, kind, k, src, dst, device):
        return pltpu.make_async_remote_copy(
            src_ref=src, dst_ref=dst, send_sem=s.sem.at[way, kind, 0, k],
            recv_sem=s.sem.at[way, kind, 1, k], device_id=device, device_id_type=MESH,
        )

    def to_sib(way, k):
        return ship(way, 0, k, s.add.at[way, 2 * k + 1 - tp], s.sib_add.at[way, k], sib)

    def to_pair(way, k):
        return ship(way, 1, k, s.chip_add.at[way, k], s.peer_add.at[way, k], ypeer)

    def along(way, k):
        device = {"ctx": ctx + (2 if way == 0 else -2)}
        return ship(way, 2, k, s.going.at[way, k], s.came.at[way, k], device)

    def start_ref(way, j):
        return (s.xs if way == 0 else s.qg).at[j, T : 2 * T, :]

    def back_to_sib(way, k):
        return ship(way, 3, k, s.sib_start.at[way, k], start_ref(way, 2 * k + tp), sib)

    def before(way):
        return lower_level if way == 0 else upper_level

    def after(way):
        return upper_level if way == 0 else lower_level

    def decays(j):
        own = s.rows[j, 1:2, :]
        theirs = s.peer_rows[j]
        return own, theirs[0:1], theirs[1:2] * theirs[2:3]

    def merge_chip(way, k):
        to_sib(way, k).wait_recv()
        j = 2 * k + tp
        own, other, _ = decays(j)
        first = tp == way
        ca = jnp.where(first, other, 1.0)
        cb = jnp.where(first, 1.0, own)
        a, b = s.add[way, j].astype(f32), s.sib_add[way, k].astype(f32)
        s.chip_add[way, k] = (ca * a + cb * b).astype(bf16)
        to_pair(way, k).start()

    def merge_level(way, k):
        j = 2 * k + tp
        own, other, d_peer = decays(j)
        d_chip = own * other
        y_first = side == way
        t_first = tp == way
        to_pair(way, k).wait_recv()
        pl.when(before(way))(lambda: along(way, k).wait_recv())
        base = s.came[way, k].astype(f32)
        mine, theirs = s.chip_add[way, k].astype(f32), s.peer_add[way, k].astype(f32)
        out = (
            (d_chip * d_peer) * base
            + jnp.where(y_first, d_peer, 1.0) * mine
            + jnp.where(y_first, 1.0, d_chip) * theirs
        )
        s.going[way, k] = out.astype(bf16)
        pl.when(after(way))(lambda: along(way, k).start())
        chip = jnp.where(y_first, 1.0, d_peer) * base + jnp.where(y_first, 0.0, theirs)
        a, b = s.add[way, j].astype(f32), s.sib_add[way, k].astype(f32)
        later = jnp.where(t_first, own, other) * chip + jnp.where(t_first, a, b)
        s.sib_start[way, k] = jnp.where(t_first, later, chip).astype(bf16)
        back_to_sib(way, k).start()
        start_ref(way, j)[...] = jnp.where(t_first, chip, later).astype(bf16)

    for way in range(2):
        @pl.when(jnp.logical_not(before(way)))
        def _():
            s.came[way] = jnp.zeros(s.came.shape[1:], bf16)

    def start_group(g):
        at_g = pl.ds(pl.multiple_of(g * STATE, STATE), STATE)
        at_b = pl.ds(pl.multiple_of(W + g * STATE, STATE), STATE)
        at_c = pl.ds(pl.multiple_of(W + N + g * STATE, STATE), STATE)
        ub = conv_pre(0, s.b[:, at_g].astype(f32), s.tail[:, at_b], s.wb[:, at_g])
        uc = conv_pre(1, s.c[:, at_g].astype(f32), s.tail[:, at_c], s.wc[:, at_g])
        s.ub[g] = ub
        s.uc[g] = uc
        bb, cb = (ub * sigmoid(ub)).astype(bf16), (uc * sigmoid(uc)).astype(bf16)
        s.bc[g] = bb
        s.cc[g] = cb
        scores = dot(cb, bb, 1, 1) * s.mask[...]
        ba, cr = bb.astype(f32) * s.end_alive[...], cb.astype(f32) * s.start_alive[...]
        s.gcr[g] = jnp.concatenate([scores, cr], axis=1).astype(bf16)
        s.gtb[g] = jnp.concatenate([scores.T, ba], axis=1).astype(bf16)
        s.bat[g] = ba.T.astype(bf16)
        s.crt[g] = cr.T.astype(bf16)

    def phase_conv(k):
        g = lax.div(k, per)
        pl.when(lax.rem(k, per) == 0)(lambda: start_group(g))
        for jj in range(2):
            j = 2 * k + jj
            weight = dot(s.whl[...], s.sel[j])
            for i in range(2):
                at_x = lanes(j, i)
                u = conv_pre(i, s.x[:, at_x].astype(f32), s.tail[:, at_x], s.wx[:, at_x])
                s.us[j, :, cols(i)] = u
                xc = (u * sigmoid(u)).astype(bf16)
                s.xc[j, :, cols(i)] = xc
                s.xs[j, 0:T, cols(i)] = (xc.astype(f32) * weight[:, cols(i)]).astype(bf16)
            s.add[0, j] = (dot(s.bat[g], s.xs[j, 0:T, :]) * s.rows[j, 0:1, :]).astype(bf16)
        to_sib(0, k).start()

    def run(lag, first, second):
        def body(k, carry):
            pl.when(k < K)(lambda: first(k))
            pl.when(k >= lag)(lambda: second(k - lag))
            return carry

        lax.fori_loop(0, K + lag, body, 0)

    for t in tells:
        t.wait_recv()
    theirs = jnp.concatenate(
        [s.dec_in[i, 0:1, :H] for i in range(3)] + [jnp.zeros((5, H), f32)], axis=0
    )
    theirs = jnp.concatenate(two(theirs), axis=1)

    def spread_peers(j, carry):
        s.peer_rows[j] = dot(theirs, s.sel[j])
        return carry

    lax.fori_loop(0, C, spread_peers, 0)

    run(1, phase_conv, partial(merge_chip, 0))

    loads[12].wait()
    s.sq[...] = jnp.zeros(s.sq.shape, f32)
    s.nu[...] = jnp.zeros(s.nu.shape, f32)

    def phase_mix(k):
        g = lax.div(k, per)
        back_to_sib(0, k).wait_recv()
        for jj in range(2):
            j = 2 * k + jj
            yr = dot(s.gcr[g], s.xs[j])
            s.yr[j] = yr
            reach = dot(s.ehl[...], s.sel[j])
            for i in range(2):
                at_x = lanes(j, i)
                m = reach[:, cols(i)] * yr[:, cols(i)]
                m = m + s.rows[j, 2:3, cols(i)] * s.xc[j, :, cols(i)].astype(f32)
                z = s.z[:, at_x].astype(f32)
                gated = m * (z * sigmoid(z))
                s.sq[...] += gated * gated
                s.nu[...] += gated * s.gw[:, at_x]

    run(1, partial(merge_level, 0), phase_mix)

    squares = jnp.sum(s.sq[...], axis=1, keepdims=True)
    numer = jnp.sum(s.nu[...], axis=1, keepdims=True)
    rms = jnp.sqrt(squares / W + epsilon)
    values = numer / rms
    vscale = (values - s.target[...]) / rms
    s.vs[...] = vscale
    s.co[...] = jnp.broadcast_to(values / (rms * W), (T, LANES))
    s.vals[...] = jnp.sum(jnp.where(eye, values, 0.0), axis=0, keepdims=True)

    stores = []

    def store(src, dst, i):
        copy = pltpu.make_async_copy(src, dst, s.out_sem.at[i])
        copy.start()
        stores.append(copy)

    store(s.vals, s.o_values, K)

    s.h1[...] = jnp.zeros(s.h1.shape, f32)
    s.h2[...] = jnp.zeros(s.h2.shape, f32)

    def head_sums(pieces, j):
        high, low_part = two(jnp.concatenate(pieces, axis=1))
        return dot(high, s.sel[j], 1, 1) + dot(low_part, s.sel[j], 1, 1)

    def phase_back(k):
        g = lax.div(k, per)
        for jj in range(2):
            j = 2 * k + jj
            reach = dot(s.ehl[...], s.sel[j])
            pieces = []
            for i in range(2):
                at_x = lanes(j, i)
                e, yr = reach[:, cols(i)], s.yr[j, :, cols(i)]
                m = e * yr + s.rows[j, 2:3, cols(i)] * s.xc[j, :, cols(i)].astype(f32)
                z = s.z[:, at_x].astype(f32)
                sg = sigmoid(z)
                gate = z * sg
                gated = m * gate
                dg = s.vs[...] * (s.gw[:, at_x] - s.co[...] * gated)
                s.gz[:, at_x] = (dg * m * (sg + gate * (1.0 - sg))).astype(bf16)
                dy = dg * gate
                s.dy[j, :, cols(i)] = dy
                q = (e * dy).astype(bf16)
                s.qg[j, 0:T, cols(i)] = q
                pieces.append(q.astype(f32) * yr)
            s.h2[...] += head_sums(pieces, j)
            s.add[1, j] = dot(s.crt[g], s.qg[j, 0:T, :]).astype(bf16)
        to_sib(1, k).start()

    run(1, phase_back, partial(merge_chip, 1))
    store(s.gz, s.o_gz, K + 1)

    def edge(k):
        return pltpu.make_async_remote_copy(
            src_ref=s.edge_out.at[k], dst_ref=s.edge_in.at[k], send_sem=s.edge_sem.at[0, k],
            recv_sem=s.edge_sem.at[1, k], device_id=prev_block, device_id_type=MESH,
        )

    def gx_part(k):
        at_k = pl.ds(pl.multiple_of(k * 2 * WIDE, 2 * WIDE), 2 * WIDE)
        return pltpu.make_async_copy(
            s.gx.at[0 : T - 16, at_k], s.o_gx.at[0 : T - 16, at_k], s.out_sem.at[k]
        )

    def finish(k, i, slot, g, u, w, out, at_o):
        head_rows, grad = conv_back(slot, silu_back(g, u), w)
        s.edge_out[k, :, cols(i)] = head_rows
        s.last[k, :, cols(i)] = grad[T - 16 :, :]
        out[:, at_o] = grad.astype(bf16)

    def phase_scores(g):
        both = jnp.zeros((T, 2 * T), f32)
        for q in range(2 * per):
            j = 2 * per * g + q
            both = both + dot(s.qg[j, 0:T, :], s.xs[j], 1, 1)
        ds = (both[:, :T] * s.mask[...]).astype(bf16)
        dc = dot(ds, s.bc[g]) + both[:, T:] * s.start_alive[...]
        s.dbs[g] = dot(ds, s.cc[g], 0, 0)
        at_g = pl.ds(pl.multiple_of(g * STATE, STATE), STATE)
        finish(per * g + per - 1, 5, 1, dc, s.uc[g], s.wc[:, at_g], s.gc, at_g)

    def phase_last(k):
        g = lax.div(k, per)
        back_to_sib(1, k).wait_recv()

        @pl.when(lax.rem(k, per) == 0)
        def _():
            s.dbacc[...] = jnp.zeros(s.dbacc.shape, f32)

        for jj in range(2):
            j = 2 * k + jj
            gam = s.qg[j, T : 2 * T, :].astype(f32)
            end = s.add[0, j].astype(f32) + s.rows[j, 1:2, :] * s.xs[j, T : 2 * T, :].astype(f32)
            s.ends[j] = jnp.sum((gam * end).reshape(STATE // 8, 8, WIDE), axis=0)
            ge = (gam * s.rows[j, 0:1, :]).astype(bf16)
            s.qg[j, T : 2 * T, :] = ge
            dxw = dot(s.gtb[g], s.qg[j])
            s.dbacc[...] += dot(s.xs[j, 0:T, :], ge, 1, 1)
            s.h1[...] += head_sums([s.xs[j, 0:T, :].astype(f32) * dxw], j)
            dx = dot(s.whl[...], s.sel[j]) * dxw + s.rows[j, 2:3, :] * s.dy[j]
            for i in range(2):
                at_x = lanes(j, i)
                finish(
                    k, 2 * jj + i, i, dx[:, cols(i)], s.us[j, :, cols(i)], s.wx[:, at_x], s.gx, at_x
                )

        @pl.when(lax.rem(k, per) == per - 1)
        def _():
            db = s.dbs[g] + s.dbacc[...] * s.end_alive[...]
            at_g = pl.ds(pl.multiple_of(g * STATE, STATE), STATE)
            finish(k, 4, 0, db, s.ub[g], s.wb[:, at_g], s.gb, at_g)

        pl.when(has_prev)(lambda: edge(k).start())
        gx_part(k).start()

    def scores_beside(k):
        merge_level(1, k)
        pl.when(lax.rem(k, per) == 0)(lambda: phase_scores(lax.div(k, per)))

    for k in range(K):
        s.edge_out[k, :, 4 * LANES :] = jnp.zeros((8, 2 * LANES), f32)
        s.last[k, :, 4 * LANES :] = jnp.zeros((16, 2 * LANES), f32)

    run(1, scores_beside, phase_last)

    h1 = s.h1[:, :H]
    dcum = s.h2[:, :H] - h1

    def end_sum(j, acc):
        high, low_part = two(s.ends[j])
        return acc + dot(high, s.sel[j], 1, 1) + dot(low_part, s.sel[j], 1, 1)

    at_end = lax.fori_loop(0, C, end_sum, jnp.zeros((8, 2 * H), f32))
    at_end = jnp.sum(at_end, axis=0, keepdims=True)[:, :H]
    upper = jnp.where(row_i <= col_i, 1.0, 0.0).astype(bf16)
    ddt = h1 / s.dt[...] - s.heads[0:1, :] * (exact_dot(upper, dcum) + at_end)
    s.gdt[...] = (ddt * sigmoid(s.dtp[...])).astype(bf16)
    store(s.gdt, s.o_gdt, K + 2)

    @pl.when(jnp.logical_not(has_next))
    def _():
        s.edge_in[...] = jnp.zeros(s.edge_in.shape, f32)

    def fix(k, carry):
        pl.when(has_next)(lambda: edge(k).wait_recv())
        share = jnp.concatenate([jnp.zeros((8, 6 * LANES), f32), s.edge_in[k]], axis=0)
        fixed = (s.last[k] + share * s.keep[:, 0:1]).astype(bf16)
        at_k = pl.ds(pl.multiple_of(k * 2 * WIDE, 2 * WIDE), 2 * WIDE)
        s.gx[T - 16 : T, at_k] = fixed[:, : 2 * WIDE]

        @pl.when(lax.rem(k, per) == per - 1)
        def _():
            at_g = pl.ds(pl.multiple_of(lax.div(k, per) * STATE, STATE), STATE)
            s.gb[T - 16 : T, at_g] = fixed[:, 2 * WIDE : 2 * WIDE + LANES]
            s.gc[T - 16 : T, at_g] = fixed[:, 2 * WIDE + LANES :]

        return carry

    lax.fori_loop(0, K, fix, 0)
    store(s.gx.at[T - 16 : T, :], s.o_gx.at[T - 16 : T, :], K + 3)
    store(s.gb, s.o_gb, K + 4)
    store(s.gc, s.o_gc, K + 5)

    def finish_sends(k, carry):
        for way in range(2):
            to_sib(way, k).wait_send()
            to_pair(way, k).wait_send()
            pl.when(after(way))(lambda: along(way, k).wait_send())
            back_to_sib(way, k).wait_send()
        pl.when(has_prev)(lambda: edge(k).wait_send())
        gx_part(k).wait()
        return carry

    lax.fori_loop(0, K, finish_sends, 0)
    for t in tells:
        t.wait_send()
    pl.when(has_next)(lambda: halo.wait_send())
    for copy in stores:
        copy.wait()


def shards(
    x_in, b_in, c_in, z_in, dt_raw, conv_x, conv_b, conv_c, decay_rate, dt_bias, skip_scale,
    norm_gain, w_value, resets, bucket, return_table,
):
    T, W = x_in.shape
    N, H = b_in.shape[1], dt_raw.shape[1]
    tn = return_table.shape[0]
    tpn = lax.axis_size("tp")
    head_rows = jnp.stack([decay_rate, dt_bias, skip_scale])
    chan_rows = jnp.stack([norm_gain, w_value])
    args = (
        x_in, b_in, c_in, z_in, dt_raw, conv_x, conv_b, conv_c, head_rows, chan_rows,
        resets.reshape(tpn, T), bucket.reshape(tpn, T), return_table[None, :],
    )
    table = scratch_table(T, W, N, H, tn)
    anywhere = pl.BlockSpec(memory_space=pl.ANY)
    values, gx, gb, gc, gz, gdt = pl.pallas_call(
        partial(kernel, lax.axis_size("ctx"), tn, (T, W, N, H), tuple(table)),
        out_shape=[
            jax.ShapeDtypeStruct((1, T), f32), jax.ShapeDtypeStruct((T, W), bf16),
            jax.ShapeDtypeStruct((T, N), bf16), jax.ShapeDtypeStruct((T, N), bf16),
            jax.ShapeDtypeStruct((T, W), bf16), jax.ShapeDtypeStruct((T, H), bf16),
        ],
        in_specs=[anywhere] * len(args),
        out_specs=[anywhere] * 6,
        scratch_shapes=list(table.values()),
        compiler_params=pltpu.CompilerParams(
            collective_id=0, has_side_effects=True, vmem_limit_bytes=58 * 1024 * 1024
        ),
    )(*args)
    return values.reshape(T), gx, gb, gc, gz, gdt


def solution(mesh):
    row = P(("group", "ctx", "tp"), None)
    seq = P(("group", "ctx"))
    return jax.shard_map(
        shards,
        mesh=mesh,
        in_specs=(row,) * 5 + (P(),) * 8 + (seq, seq, P()),
        out_specs=(P(("group", "ctx", "tp")),) + (row,) * 5,
        check_vma=False,
    )
```

```python
from functools import partial

import jax
import jax.numpy as jnp
import numpy as np
from jax import lax
from jax.experimental import pallas as pl
from jax.experimental.pallas import tpu as pltpu
from jax.sharding import PartitionSpec as P

HEAD_DIM = 64
STATE = 128
LANES = 128
WIDE = 256
MESH = pl.DeviceIdType.MESH
F_LAG, F_WAIT, F_SPLIT, F_MIX = 5, 3, 3, 4
B_LAG, B_WAIT, B_LAST, B_SPLIT, B_OUT, B_LAST_OUT = 5, 3, 4, 3, 8, 4

epsilon = 1e-05
f32 = jnp.float32
bf16 = jnp.bfloat16


def dot(a, b, ca=1, cb=0):
    return lax.dot_general(a, b, (((ca,), (cb,)), ((), ())), preferred_element_type=f32)


def sigmoid(u):
    return 1.0 / (1.0 + jnp.exp(-u))


def iota(shape, dim):
    return lax.broadcasted_iota(jnp.int32, shape, dim)


def two(v):
    high = v.astype(bf16)
    return high, (v - high.astype(f32)).astype(bf16)


def three(v):
    high = v.astype(bf16)
    rest = v - high.astype(f32)
    middle = rest.astype(bf16)
    return high, middle, (rest - middle.astype(f32)).astype(bf16)


def exact_dot(select, v):
    return sum(dot(select, part) for part in three(v))


def twice(v):
    return jnp.concatenate([v, v], axis=1)


INPUTS = (
    "x_in", "b_in", "c_in", "z_in", "dt_in", "conv_x", "conv_b", "conv_c", "rate_in", "bias_in",
    "skip_in", "gain_in", "value_in", "resets", "bucket", "table", "sel_in",
)
OUTPUTS = (
    "o_values", "o_gx", "o_gb", "o_gc", "o_gz", "o_gdt",
)


def scratch_table(T, W, N, H, tn):
    G, C = N // STATE, W // WIDE
    K = C // 2
    per = K // G
    V, D, R = pltpu.VMEM, pltpu.SemaphoreType.DMA, pltpu.SemaphoreType.REGULAR
    return dict(
        x=V((T, W), bf16), b=V((T, N), bf16), c=V((T, N), bf16), z=V((T, W), bf16),
        dt_raw=V((H, T), bf16), wx=V((4, W), f32), wb=V((4, N), f32), wc=V((4, N), f32),
        rate=V((1, H), f32), bias=V((1, H), f32), skip=V((1, H), f32),
        gain=V((1, W), f32), value=V((1, W), f32), rs=V((2, T), jnp.int32),
        xt=V((16, W), bf16), bt=V((16, N), bf16), ct=V((16, N), bf16),
        bk=V((2, T), jnp.int32), tab=V((1, tn), f32),
        vals=V((1, T), f32), gx=V((T, W), bf16), gb=V((T, N), bf16), gc=V((T, N), bf16),
        gz=V((T, W), bf16), gdt=V((H, T), bf16),
        halo_out=V((16, (W + 2 * N) // 4), bf16), halo_in=V((16, (W + 2 * N) // 4), bf16),
        halo_wide=V((16, (W + 2 * N) // 4), f32),
        tail=V((8, W + 2 * N), f32),
        edge_out=V((K, 8, 6 * LANES), f32), edge_in=V((K, 8, 6 * LANES), f32),
        last=V((K, 16, 6 * LANES), f32),
        dec_out=V((8, LANES), f32), dec_in=V((3, 8, LANES), f32),
        valid=V((3, T, LANES), f32), shifted=V((3, T + 8, LANES), f32),
        mask=V((T, T), f32), start_alive=V((T, LANES), f32), end_alive=V((T, LANES), f32),
        keep=V((16, LANES), f32), target=V((T, LANES), f32),
        pos=V((T + 8, LANES), f32),
        dt=V((T, H), f32), dtp=V((T, H), f32),
        ehl=V((T, 2 * H), bf16), whl=V((T, 2 * H), bf16),
        sel=V((C, 2 * H, WIDE), bf16), rows=V((C, 8, WIDE), f32),
        peer_rows=V((C, 8, WIDE), f32), gw=V((1, W), f32),
        ext=V((2, T + 8, LANES), f32), back=V((2, T + 16, LANES), f32),
        us=V((C, T, WIDE), f32), xc=V((C, T, WIDE), bf16), xs=V((C, 2 * T, WIDE), bf16),
        qg=V((C, 2 * T, WIDE), bf16), yr=V((C, T, WIDE), f32), dy=V((C, T, WIDE), f32),
        ub=V((G, T, STATE), f32), uc=V((G, T, STATE), f32),
        bc=V((G, T, STATE), bf16), cc=V((G, T, STATE), bf16),
        gcr=V((G, T, 2 * T), bf16), gtb=V((G, T, 2 * T), bf16),
        bat=V((G, STATE, T), bf16), crt=V((G, STATE, T), bf16),
        dbs=V((G, T, STATE), f32), dbacc=V((T, STATE), f32),
        sq=V((T, LANES), f32), nu=V((T, LANES), f32),
        vs=V((T, LANES), f32), co=V((T, LANES), f32),
        h1=V((T + 16, 2 * H), f32), h2=V((T, 2 * H), f32), end=V((C, STATE, WIDE), bf16),
        add=V((2, C, STATE, WIDE), bf16), sib_add=V((2, K, STATE, WIDE), bf16),
        chip_add=V((2, K, STATE, WIDE), bf16), peer_add=V((2, K, STATE // 2, WIDE), bf16),
        going=V((2, K, STATE // 2, WIDE), bf16), came=V((2, K, STATE // 2, WIDE), bf16),
        pair_start=V((2, K, STATE // 2, WIDE), bf16), chip_start=V((2, K, STATE, WIDE), bf16),
        sib_start=V((2, K, STATE, WIDE), bf16),
        in_sem=D((20,)), out_sem=D((K + 6,)), halo_sem=D((2,)), dec_sem=D((2, 3)),
        edge_sem=D((2, K)), sem=D((2, 5, 2, K)),
    )


def kernel(cn, tn, dims, names, *refs):
    r = dict(zip(list(INPUTS) + list(OUTPUTS) + list(names), refs))

    class Bag:
        pass

    s = Bag()
    for key, ref in r.items():
        setattr(s, key, ref)
    T, W, N, H = dims
    G, C = N // STATE, W // WIDE
    K = C // 2
    per = K // G

    ctx, tp = lax.axis_index("ctx"), lax.axis_index("tp")
    side = lax.rem(ctx, 2)
    peer = ctx + 1 - 2 * side
    sib = {"tp": 1 - tp}
    ypeer = {"ctx": peer}
    yother = {"ctx": peer, "tp": 1 - tp}
    level, levels = lax.div(ctx, 2), cn // 2
    lower_level, upper_level = level > 0, level < levels - 1
    next_block = {"ctx": ctx + tp, "tp": 1 - tp}
    prev_block = {"ctx": ctx - 1 + tp, "tp": 1 - tp}
    has_next = jnp.logical_or(tp == 0, ctx < cn - 1)
    has_prev = jnp.logical_or(tp == 1, ctx > 0)
    cross_next = jnp.logical_and(tp == 1, ctx < cn - 1)
    cross_prev = jnp.logical_and(tp == 0, ctx > 0)

    last_rows = slice(T - 16, T)
    load = {}

    def loader(src, dst, i):
        return lambda: pltpu.make_async_copy(src, dst, s.in_sem.at[i])

    for i, (name, src, dst) in enumerate([
        ("rs", s.resets, s.rs), ("xt", s.x_in.at[last_rows], s.xt),
        ("bt", s.b_in.at[last_rows], s.bt), ("ct", s.c_in.at[last_rows], s.ct),
        ("dt", s.dt_in, s.dt_raw), ("rate", s.rate_in, s.rate), ("bias", s.bias_in, s.bias),
        ("skip", s.skip_in, s.skip), ("sel", s.sel_in, s.sel), ("b", s.b_in, s.b),
        ("c", s.c_in, s.c), ("wb", s.conv_b, s.wb), ("wc", s.conv_c, s.wc), ("x", s.x_in, s.x),
        ("wx", s.conv_x, s.wx), ("z", s.z_in, s.z), ("gain", s.gain_in, s.gain),
        ("value", s.value_in, s.value), ("bk", s.bucket, s.bk), ("tab", s.table, s.tab),
    ]):
        load[name] = loader(src, dst, i)
        load[name]().start()

    def loaded(*which):
        for name in which:
            load[name]().wait()

    barrier = pltpu.get_barrier_semaphore()

    def greet(device):
        pl.semaphore_signal(barrier, inc=1, device_id=device, device_id_type=MESH)

    greet(sib)
    greet(ypeer)
    greet(yother)
    pl.when(upper_level)(lambda: greet({"ctx": ctx + 2}))
    pl.when(lower_level)(lambda: greet({"ctx": ctx - 2}))
    pl.when(cross_next)(lambda: greet(next_block))
    pl.when(cross_prev)(lambda: greet(prev_block))

    def one(flag):
        return jnp.where(flag, 1, 0)

    row_i, col_i = iota((T, T), 0), iota((T, T), 1)
    eye = row_i == col_i
    lower = row_i >= col_i

    def column(row):
        return jnp.sum(jnp.where(eye, row, 0.0), axis=1, keepdims=True)

    loaded("rs")
    real = jnp.broadcast_to(column(s.rs[pl.ds(tp, 1), :].astype(f32)), (T, LANES))
    s.pos[0:8, :] = jnp.zeros((8, LANES), f32)
    s.pos[8 : 8 + T, :] = real
    last_r = s.pos[T + 7 : T + 8, :]
    last_two = jnp.maximum(last_r, s.pos[T + 6 : T + 7, :])
    at = iota((16, LANES), 0)
    keep = jnp.where(at == 13, 1.0 - last_two, jnp.where(at == 14, 1.0 - last_r, 1.0))
    s.keep[...] = keep
    keep8 = keep[8:16, 0:1]

    loaded("xt", "bt", "ct")
    ends = [ref[...].astype(f32)[8:16] * keep8 for ref in (s.xt, s.bt, s.ct)]
    ends = jnp.concatenate(ends, axis=1)
    quarter = (W + 2 * N) // 4
    for q in range(4):
        s.halo_wide[4 * q : 4 * q + 4, :] = ends[4:8, q * quarter : (q + 1) * quarter]
    s.halo_out[...] = s.halo_wide[...].astype(bf16)
    pl.semaphore_wait(
        barrier, 3 + one(upper_level) + one(lower_level) + one(cross_next) + one(cross_prev)
    )
    halo = pltpu.make_async_remote_copy(
        src_ref=s.halo_out, dst_ref=s.halo_in, send_sem=s.halo_sem.at[0],
        recv_sem=s.halo_sem.at[1], device_id=next_block, device_id_type=MESH,
    )
    pl.when(has_next)(lambda: halo.start())

    loaded("dt", "rate", "bias", "skip")
    rate, skip = s.rate[...], s.skip[...]
    dtp = s.dt_raw[...].astype(f32).T + s.bias[...]
    dt = jnp.maximum(dtp, 0.0) + jnp.log1p(jnp.exp(-jnp.abs(dtp)))
    s.dtp[...] = dtp
    s.dt[...] = dt
    low = jnp.where(lower, 1.0, 0.0).astype(bf16)
    cum = exact_dot(low, -dt * rate)
    counts = dot(low, real.astype(bf16))
    total = counts[T - 1 : T, :]
    cum_end = cum[T - 1 : T, :]
    eend = jnp.exp(cum_end)
    decay = eend * jnp.where(total[:, :H] == 0.0, 1.0, 0.0)
    s.dec_out[...] = jnp.broadcast_to(twice(decay), (8, 2 * H))

    def tell(i, device):
        return pltpu.make_async_remote_copy(
            src_ref=s.dec_out, dst_ref=s.dec_in.at[i], send_sem=s.dec_sem.at[0, i],
            recv_sem=s.dec_sem.at[1, i], device_id=device, device_id_type=MESH,
        )

    tells = [tell(0, sib), tell(1, ypeer), tell(2, yother)]
    for t in tells:
        t.start()

    s.mask[...] = jnp.where(jnp.logical_and(lower, counts == counts.T), 1.0, 0.0)
    s.start_alive[...] = jnp.where(counts == 0.0, 1.0, 0.0)
    s.end_alive[...] = jnp.where(counts == total, 1.0, 0.0)
    one_back, two_back = s.pos[7 : 7 + T, :], s.pos[6 : 6 + T, :]
    second = jnp.maximum(real, one_back)
    for k, flag in enumerate([real, second, jnp.maximum(second, two_back)]):
        s.valid[k] = 1.0 - flag
    for k in range(3):
        m = k + 1
        s.shifted[k, 0:8, :] = jnp.zeros((8, LANES), f32)
        s.shifted[k, T : T + 8, :] = jnp.zeros((8, LANES), f32)
        s.shifted[k, 8 - m : 8 - m + T, :] = s.valid[k]
    for i in range(2):
        s.back[i, 0:8, :] = jnp.zeros((8, LANES), f32)
        s.back[i, T + 8 : T + 16, :] = jnp.zeros((8, LANES), f32)
    s.ehl[...] = jnp.concatenate(two(jnp.exp(cum)), axis=1)
    s.whl[...] = jnp.concatenate(two(jnp.exp(-cum) * dt), axis=1)

    def spread(rows, out):
        halves = jnp.concatenate(two(rows), axis=1)
        for j in range(C):
            out[j] = dot(halves, s.sel[j])

    loaded("sel")
    spread(jnp.concatenate([eend, decay, skip] + [jnp.zeros((1, H), f32)] * 5, axis=0), s.rows)
    loaded("b", "c", "wb", "wc", "x", "wx")

    @pl.when(has_prev)
    def _():
        halo.wait_recv()

    @pl.when(jnp.logical_not(has_prev))
    def _():
        s.halo_in[...] = jnp.zeros(s.halo_in.shape, bf16)

    s.halo_wide[...] = s.halo_in[...].astype(f32)
    for q in range(4):
        s.tail[4:8, q * quarter : (q + 1) * quarter] = s.halo_wide[4 * q : 4 * q + 4, :]

    def conv_pre(slot, piece, tail, w):
        ext = s.ext.at[slot]
        ext[0:8, :] = tail
        ext[8 : 8 + T, :] = piece
        u = w[0:1] * piece
        for k in range(1, 4):
            u = u + (w[k : k + 1] * ext[8 - k : 8 - k + T, :]) * s.valid[k - 1]
        return u

    def conv_back(slot, du, w):
        ext = s.back.at[slot]
        ext[8 : 8 + T, :] = du
        g = w[0:1] * ext[0 : T + 8, :]
        for k in range(1, 4):
            g = g + (w[k : k + 1] * ext[k : k + T + 8, :]) * s.shifted[k - 1]
        return g[0:8], g[8:]

    def silu_both(u):
        sg = sigmoid(u)
        value = u * sg
        return value.astype(bf16), sg + value * (1.0 - sg)

    def lanes(j, i):
        return pl.ds(pl.multiple_of(j * WIDE + i * LANES, LANES), LANES)

    def cols(i):
        return slice(i * LANES, (i + 1) * LANES)

    HALF = STATE // 2
    own_half = pl.ds(pl.multiple_of(side * HALF, HALF), HALF)
    pair_half = pl.ds(pl.multiple_of((1 - side) * HALF, HALF), HALF)

    def ship(way, kind, k, src, dst, device):
        return pltpu.make_async_remote_copy(
            src_ref=src, dst_ref=dst, send_sem=s.sem.at[way, kind, 0, k],
            recv_sem=s.sem.at[way, kind, 1, k], device_id=device, device_id_type=MESH,
        )

    def to_sib(way, k):
        return ship(way, 0, k, s.add.at[way, 2 * k + 1 - tp], s.sib_add.at[way, k], sib)

    def to_pair(way, k):
        return ship(way, 1, k, s.chip_add.at[way, k, pair_half], s.peer_add.at[way, k], ypeer)

    def along(way, k):
        device = {"ctx": ctx + (2 if way == 0 else -2)}
        return ship(way, 2, k, s.going.at[way, k], s.came.at[way, k], device)

    def back_to_pair(way, k):
        return ship(
            way, 3, k, s.pair_start.at[way, k], s.chip_start.at[way, k, own_half], ypeer
        )

    def start_ref(way, j):
        return (s.xs if way == 0 else s.qg).at[j, T : 2 * T, :]

    def back_to_sib(way, k):
        return ship(way, 4, k, s.sib_start.at[way, k], start_ref(way, 2 * k + tp), sib)

    def before(way):
        return lower_level if way == 0 else upper_level

    def after(way):
        return upper_level if way == 0 else lower_level

    def decays(j):
        own = s.rows[j, 1:2, :]
        theirs = s.peer_rows[j]
        return own, theirs[0:1], theirs[1:2] * theirs[2:3]

    def merge_chip(way, k):
        to_sib(way, k).wait_recv()
        j = 2 * k + tp
        own, other, _ = decays(j)
        first = tp == way
        ca = jnp.where(first, other, 1.0)
        cb = jnp.where(first, 1.0, own)
        a, b = s.add[way, j].astype(f32), s.sib_add[way, k].astype(f32)
        s.chip_add[way, k] = (ca * a + cb * b).astype(bf16)
        to_pair(way, k).start()

    def merge_level(way, k):
        own, other, d_peer = decays(2 * k + tp)
        d_chip = own * other
        y_first = side == way
        to_pair(way, k).wait_recv()
        pl.when(before(way))(lambda: along(way, k).wait_recv())
        base = jnp.where(before(way), s.came[way, k].astype(f32), 0.0)
        mine = s.chip_add[way, k, own_half, :].astype(f32)
        theirs = s.peer_add[way, k].astype(f32)
        d_first = jnp.where(y_first, d_chip, d_peer)
        d_last = jnp.where(y_first, d_peer, d_chip)
        middle = d_first * base + jnp.where(y_first, mine, theirs)
        out = d_last * middle + jnp.where(y_first, theirs, mine)
        s.going[way, k] = out.astype(bf16)
        pl.when(after(way))(lambda: along(way, k).start())
        s.pair_start[way, k] = jnp.where(y_first, middle, base).astype(bf16)
        back_to_pair(way, k).start()
        s.chip_start[way, k, own_half, :] = jnp.where(y_first, base, middle).astype(bf16)

    def split_chip(way, k):
        back_to_pair(way, k).wait_recv()
        j = 2 * k + tp
        own, other, _ = decays(j)
        t_first = tp == way
        chip = s.chip_start[way, k].astype(f32)
        ahead = jnp.where(t_first, s.add[way, j], s.sib_add[way, k]).astype(f32)
        later = (jnp.where(t_first, own, other) * chip + ahead).astype(bf16)
        chip = s.chip_start[way, k]
        s.sib_start[way, k] = jnp.where(t_first, later, chip)
        back_to_sib(way, k).start()
        start_ref(way, j)[...] = jnp.where(t_first, chip, later)

    def start_group(g):
        at_g = pl.ds(pl.multiple_of(g * STATE, STATE), STATE)
        at_b = pl.ds(pl.multiple_of(W + g * STATE, STATE), STATE)
        at_c = pl.ds(pl.multiple_of(W + N + g * STATE, STATE), STATE)
        ub = conv_pre(0, s.b[:, at_g].astype(f32), s.tail[:, at_b], s.wb[:, at_g])
        uc = conv_pre(1, s.c[:, at_g].astype(f32), s.tail[:, at_c], s.wc[:, at_g])
        bb, s.ub[g] = silu_both(ub)
        cb, s.uc[g] = silu_both(uc)
        s.bc[g] = bb
        s.cc[g] = cb
        scores = dot(cb, bb, 1, 1) * s.mask[...]
        ba, cr = bb.astype(f32) * s.end_alive[...], cb.astype(f32) * s.start_alive[...]
        s.gcr[g] = jnp.concatenate([scores, cr], axis=1).astype(bf16)
        s.gtb[g] = jnp.concatenate([scores.T, ba], axis=1).astype(bf16)
        s.bat[g] = ba.T.astype(bf16)
        s.crt[g] = cr.T.astype(bf16)

    def phase_conv(k):
        g = lax.div(k, per)
        pl.when(lax.rem(k, per) == 0)(lambda: start_group(g))
        for jj in range(2):
            j = 2 * k + jj
            weight = dot(s.whl[...], s.sel[j])
            for i in range(2):
                at_x = lanes(j, i)
                u = conv_pre(i, s.x[:, at_x].astype(f32), s.tail[:, at_x], s.wx[:, at_x])
                xc, s.us[j, :, cols(i)] = silu_both(u)
                s.xc[j, :, cols(i)] = xc
                s.xs[j, 0:T, cols(i)] = (xc.astype(f32) * weight[:, cols(i)]).astype(bf16)
            s.add[0, j] = (dot(s.bat[g], s.xs[j, 0:T, :]) * s.rows[j, 0:1, :]).astype(bf16)
        to_sib(0, k).start()

    def run(steps, total):
        def body(i, carry):
            for start, count, step in steps:
                pl.when(jnp.logical_and(i >= start, i < start + count))(
                    partial(step, i - start)
                )
            return carry

        lax.fori_loop(0, total, body, 0)

    def meet_peers(_):
        for t in tells:
            t.wait_recv()
        got = [s.dec_in[i, 0:1, :H] for i in range(3)]
        spread(jnp.concatenate(got + [jnp.zeros((5, H), f32)], axis=0), s.peer_rows)

    s.sq[...] = jnp.zeros(s.sq.shape, f32)
    s.nu[...] = jnp.zeros(s.nu.shape, f32)

    def prepare_mix(_):
        loaded("z", "gain", "value", "bk", "tab")
        s.gw[...] = s.gain[...] * s.value[...]
        place = column(s.bk[pl.ds(tp, 1), :].astype(f32))
        tabled = jnp.where(place == iota((T, tn), 1).astype(f32), s.tab[...], 0.0)
        s.target[...] = jnp.broadcast_to(jnp.sum(tabled, axis=1, keepdims=True), (T, LANES))

    def phase_mix(k):
        g = lax.div(k, per)
        back_to_sib(0, k).wait_recv()
        for jj in range(2):
            j = 2 * k + jj
            yr = dot(s.gcr[g], s.xs[j])
            s.yr[j] = yr
            carried = s.rows[j, 1:2, :] * s.xs[j, T : 2 * T, :].astype(f32)
            s.end[j] = (s.add[0, j].astype(f32) + carried).astype(bf16)
            reach = dot(s.ehl[...], s.sel[j])
            for i in range(2):
                at_x = lanes(j, i)
                m = reach[:, cols(i)] * yr[:, cols(i)]
                m = m + s.rows[j, 2:3, cols(i)] * s.xc[j, :, cols(i)].astype(f32)
                z = s.z[:, at_x].astype(f32)
                gated = m * (z * sigmoid(z))
                s.sq[...] += gated * gated
                s.nu[...] += gated * s.gw[:, at_x]

    first = F_LAG + F_WAIT * one(before(0))
    run(
        [
            (first, K, partial(merge_level, 0)),
            (first + F_SPLIT, K, partial(split_chip, 0)),
            (0, K, phase_conv),
            (1, 1, meet_peers),
            (1, K, partial(merge_chip, 0)),
            (K, 1, prepare_mix),
            (first + F_MIX, K, phase_mix),
        ],
        F_LAG + F_WAIT + F_MIX + K,
    )

    squares = jnp.sum(s.sq[...], axis=1, keepdims=True)
    numer = jnp.sum(s.nu[...], axis=1, keepdims=True)
    rms = jnp.sqrt(squares / W + epsilon)
    values = numer / rms
    vscale = (values - s.target[...]) / rms
    s.vs[...] = vscale
    s.co[...] = jnp.broadcast_to(values / (rms * W), (T, LANES))
    s.vals[...] = jnp.sum(jnp.where(eye, values, 0.0), axis=0, keepdims=True)

    stores = []

    def store(src, dst, i):
        copy = pltpu.make_async_copy(src, dst, s.out_sem.at[i])
        copy.start()
        stores.append(copy)

    store(s.vals, s.o_values, K)

    s.h1[...] = jnp.zeros(s.h1.shape, f32)
    s.h2[...] = jnp.zeros(s.h2.shape, f32)

    def head_sums(v, j):
        return dot(v.astype(bf16), s.sel[j], 1, 1)

    def phase_back(k):
        g = lax.div(k, per)
        for jj in range(2):
            j = 2 * k + jj
            reach = dot(s.ehl[...], s.sel[j])
            pieces = []
            for i in range(2):
                at_x = lanes(j, i)
                e, yr = reach[:, cols(i)], s.yr[j, :, cols(i)]
                m = e * yr + s.rows[j, 2:3, cols(i)] * s.xc[j, :, cols(i)].astype(f32)
                z = s.z[:, at_x].astype(f32)
                sg = sigmoid(z)
                gate = z * sg
                gated = m * gate
                dg = s.vs[...] * (s.gw[:, at_x] - s.co[...] * gated)
                s.gz[:, at_x] = (dg * m * (sg + gate * (1.0 - sg))).astype(bf16)
                dy = dg * gate
                s.dy[j, :, cols(i)] = dy
                q = (e * dy).astype(bf16)
                s.qg[j, 0:T, cols(i)] = q
                pieces.append(q.astype(f32) * yr)
            s.h2[...] += head_sums(jnp.concatenate(pieces, axis=1), j)
            s.add[1, j] = dot(s.crt[g], s.qg[j, 0:T, :]).astype(bf16)
        to_sib(1, k).start()

    def edge(k):
        return pltpu.make_async_remote_copy(
            src_ref=s.edge_out.at[k], dst_ref=s.edge_in.at[k], send_sem=s.edge_sem.at[0, k],
            recv_sem=s.edge_sem.at[1, k], device_id=prev_block, device_id_type=MESH,
        )

    def gx_part(k):
        at_k = pl.ds(pl.multiple_of(k * 2 * WIDE, 2 * WIDE), 2 * WIDE)
        return pltpu.make_async_copy(
            s.gx.at[0 : T - 16, at_k], s.o_gx.at[0 : T - 16, at_k], s.out_sem.at[k]
        )

    def finish(k, i, slot, du, w, out, at_o):
        head_rows, grad = conv_back(slot, du, w)
        s.edge_out[k, :, cols(i)] = head_rows
        s.last[k, :, cols(i)] = grad[T - 16 :, :]
        out[:, at_o] = grad.astype(bf16)

    def phase_scores(g):
        both = jnp.zeros((T, 2 * T), f32)
        for q in range(2 * per):
            j = 2 * per * g + q
            both = both + dot(s.qg[j, 0:T, :], s.xs[j], 1, 1)
        ds = (both[:, :T] * s.mask[...]).astype(bf16)
        dc = dot(ds, s.bc[g]) + both[:, T:] * s.start_alive[...]
        s.dbs[g] = dot(ds, s.cc[g], 0, 0)
        at_g = pl.ds(pl.multiple_of(g * STATE, STATE), STATE)
        finish(per * g + per - 1, 5, 1, dc * s.uc[g], s.wc[:, at_g], s.gc, at_g)

    def phase_last(k):
        g = lax.div(k, per)
        back_to_sib(1, k).wait_recv()

        @pl.when(lax.rem(k, per) == 0)
        def _():
            s.dbacc[...] = jnp.zeros(s.dbacc.shape, f32)

        for jj in range(2):
            j = 2 * k + jj
            gam = s.qg[j, T : 2 * T, :].astype(f32)
            ends = jnp.sum((gam * s.end[j].astype(f32)).reshape(STATE // 16, 16, WIDE), axis=0)
            ge = (gam * s.rows[j, 0:1, :]).astype(bf16)
            s.qg[j, T : 2 * T, :] = ge
            dxw = dot(s.gtb[g], s.qg[j])
            s.dbacc[...] += dot(s.xs[j, 0:T, :], ge, 1, 1)
            xg = s.xs[j, 0:T, :].astype(f32) * dxw
            s.h1[...] += head_sums(jnp.concatenate([xg, ends], axis=0), j)
            dx = dot(s.whl[...], s.sel[j]) * dxw + s.rows[j, 2:3, :] * s.dy[j]
            for i in range(2):
                at_x = lanes(j, i)
                du = dx[:, cols(i)] * s.us[j, :, cols(i)]
                finish(k, 2 * jj + i, i, du, s.wx[:, at_x], s.gx, at_x)

        @pl.when(lax.rem(k, per) == per - 1)
        def _():
            db = s.dbs[g] + s.dbacc[...] * s.end_alive[...]
            at_g = pl.ds(pl.multiple_of(g * STATE, STATE), STATE)
            finish(k, 4, 0, db * s.ub[g], s.wb[:, at_g], s.gb, at_g)

        pl.when(has_prev)(lambda: edge(k).start())
        gx_part(k).start()

    for k in range(K):
        s.edge_out[k, :, 4 * LANES :] = jnp.zeros((8, 2 * LANES), f32)
        s.last[k, :, 4 * LANES :] = jnp.zeros((16, 2 * LANES), f32)

    def gz_copy():
        return pltpu.make_async_copy(s.gz, s.o_gz, s.out_sem.at[K + 1])

    last = jnp.logical_not(after(1))
    first = B_LAG + B_WAIT * one(before(1)) + B_LAST * one(last)
    scores_at = first + K - (first + K - K) * one(last)
    last_at = first + B_LAST_OUT + (B_OUT - B_LAST_OUT) * one(after(1))
    run(
        [
            (first, K, partial(merge_level, 1)),
            (first + B_SPLIT, K, partial(split_chip, 1)),
            (0, K, phase_back),
            (1, K, partial(merge_chip, 1)),
            (K, 1, lambda _: gz_copy().start()),
            (scores_at, G, phase_scores),
            (last_at, K, phase_last),
        ],
        B_LAG + B_WAIT + B_LAST + B_OUT + K,
    )

    h1 = s.h1[0:T, :H]
    dcum = s.h2[:, :H] - h1

    at_end = jnp.sum(s.h1[T : T + 16, :H], axis=0, keepdims=True)
    upper = jnp.where(row_i <= col_i, 1.0, 0.0).astype(bf16)
    ddt = h1 / s.dt[...] - s.rate[...] * (exact_dot(upper, dcum) + at_end)
    s.gdt[...] = (ddt * sigmoid(s.dtp[...])).T.astype(bf16)
    store(s.gdt, s.o_gdt, K + 2)

    @pl.when(jnp.logical_not(has_next))
    def _():
        s.edge_in[...] = jnp.zeros(s.edge_in.shape, f32)

    def fix(k, carry):
        pl.when(has_next)(lambda: edge(k).wait_recv())
        share = jnp.concatenate([jnp.zeros((8, 6 * LANES), f32), s.edge_in[k]], axis=0)
        fixed = (s.last[k] + share * s.keep[:, 0:1]).astype(bf16)
        at_k = pl.ds(pl.multiple_of(k * 2 * WIDE, 2 * WIDE), 2 * WIDE)
        s.gx[T - 16 : T, at_k] = fixed[:, : 2 * WIDE]

        @pl.when(lax.rem(k, per) == per - 1)
        def _():
            at_g = pl.ds(pl.multiple_of(lax.div(k, per) * STATE, STATE), STATE)
            s.gb[T - 16 : T, at_g] = fixed[:, 2 * WIDE : 2 * WIDE + LANES]
            s.gc[T - 16 : T, at_g] = fixed[:, 2 * WIDE + LANES :]

        return carry

    lax.fori_loop(0, K, fix, 0)
    store(s.gx.at[T - 16 : T, :], s.o_gx.at[T - 16 : T, :], K + 3)
    store(s.gb, s.o_gb, K + 4)
    store(s.gc, s.o_gc, K + 5)

    def finish_sends(k, carry):
        for way in range(2):
            to_sib(way, k).wait_send()
            to_pair(way, k).wait_send()
            pl.when(after(way))(lambda: along(way, k).wait_send())
            back_to_pair(way, k).wait_send()
            back_to_sib(way, k).wait_send()
        pl.when(has_prev)(lambda: edge(k).wait_send())
        gx_part(k).wait()
        return carry

    lax.fori_loop(0, K, finish_sends, 0)
    for t in tells:
        t.wait_send()
    pl.when(has_next)(lambda: halo.wait_send())
    gz_copy().wait()
    for copy in stores:
        copy.wait()


def pass_on(*refs):
    ins, outs, held, sems = refs[:6], refs[6:12], refs[12:18], refs[18]
    pieces = []
    for i, (a, o, h) in enumerate(zip(ins, outs, held)):
        parts = 4 if a.shape[0] * a.shape[1] > 128 * 1024 else 1
        rows = a.shape[0] // parts
        for q in range(parts):
            at = slice(q * rows, (q + 1) * rows)
            come = pltpu.make_async_copy(a.at[at], h.at[at], sems.at[0, i, q])
            go = pltpu.make_async_copy(h.at[at], o.at[at], sems.at[1, i, q])
            come.start()
            pieces.append((come, go))
    for come, go in pieces:
        come.wait()
        go.start()
    for come, go in pieces:
        go.wait()


def shards(
    x_in, b_in, c_in, z_in, dt_raw, conv_x, conv_b, conv_c, decay_rate, dt_bias, skip_scale,
    norm_gain, w_value, resets, bucket, return_table,
):
    T, W = x_in.shape
    N, H = b_in.shape[1], dt_raw.shape[1]
    tn = return_table.shape[0]
    tpn = lax.axis_size("tp")
    C = W // WIDE
    head = np.arange(2 * H)[None, :, None] % H
    lane_head = np.arange(WIDE)[None, None, :] // HEAD_DIM
    chunk_head = np.arange(C)[:, None, None] * (WIDE // HEAD_DIM)
    sel = jnp.asarray(head == lane_head + chunk_head, bf16)
    args = (
        x_in, b_in, c_in, z_in, dt_raw.T, conv_x, conv_b, conv_c, decay_rate[None, :],
        dt_bias[None, :], skip_scale[None, :], norm_gain[None, :], w_value[None, :],
        resets.reshape(tpn, T), bucket.reshape(tpn, T), return_table[None, :], sel,
    )
    table = scratch_table(T, W, N, H, tn)
    anywhere = pl.BlockSpec(memory_space=pl.ANY)
    outs = pl.pallas_call(
        partial(kernel, lax.axis_size("ctx"), tn, (T, W, N, H), tuple(table)),
        out_shape=[
            jax.ShapeDtypeStruct((1, T), f32), jax.ShapeDtypeStruct((T, W), bf16),
            jax.ShapeDtypeStruct((T, N), bf16), jax.ShapeDtypeStruct((T, N), bf16),
            jax.ShapeDtypeStruct((T, W), bf16), jax.ShapeDtypeStruct((H, T), bf16),
        ],
        in_specs=[anywhere] * len(args),
        out_specs=[anywhere] * 6,
        scratch_shapes=list(table.values()),
        compiler_params=pltpu.CompilerParams(
            collective_id=0, has_side_effects=True, vmem_limit_bytes=58 * 1024 * 1024
        ),
    )(*args)
    values, gx, gb, gc, gz, gdt = pl.pallas_call(
        pass_on,
        out_shape=[jax.ShapeDtypeStruct(o.shape, o.dtype) for o in outs],
        in_specs=[anywhere] * 6,
        out_specs=[anywhere] * 6,
        scratch_shapes=[pltpu.VMEM(o.shape, o.dtype) for o in outs]
        + [pltpu.SemaphoreType.DMA((2, 6, 4))],
    )(*outs)
    return values.reshape(T), gx, gb, gc, gz, gdt.T


def solution(mesh):
    row = P(("group", "ctx", "tp"), None)
    seq = P(("group", "ctx"))
    return jax.shard_map(
        shards,
        mesh=mesh,
        in_specs=(row,) * 5 + (P(),) * 8 + (seq, seq, P()),
        out_specs=(P(("group", "ctx", "tp")),) + (row,) * 5,
        check_vma=False,
    )
```

```python
from functools import partial

import jax
import jax.numpy as jnp
import numpy as np
from jax import lax
from jax.experimental import pallas as pl
from jax.experimental.pallas import tpu as pltpu
from jax.sharding import PartitionSpec as P

HEAD_DIM = 64
STATE = 128
LANES = 128
WIDE = 256
RING = 4
MESH = pl.DeviceIdType.MESH
F_LAG, F_WAIT, F_SPLIT, F_MIX = 6, 2, 4, 6
B_LAG, B_WAIT, B_SPLIT, B_OUT, B_SCORES = 6, 4, 4, 6, 8

epsilon = 1e-05
f32 = jnp.float32
bf16 = jnp.bfloat16


def dot(a, b, ca=1, cb=0):
    return lax.dot_general(a, b, (((ca,), (cb,)), ((), ())), preferred_element_type=f32)


def sigmoid(u):
    return 1.0 / (1.0 + jnp.exp(-u))


def iota(shape, dim):
    return lax.broadcasted_iota(jnp.int32, shape, dim)


def two(v):
    high = v.astype(bf16)
    return high, (v - high.astype(f32)).astype(bf16)


def three(v):
    high = v.astype(bf16)
    rest = v - high.astype(f32)
    middle = rest.astype(bf16)
    return high, middle, (rest - middle.astype(f32)).astype(bf16)


def exact_dot(select, v):
    return sum(dot(select, part) for part in three(v))


def twice(v):
    return jnp.concatenate([v, v], axis=1)


INPUTS = (
    "x_in", "b_in", "c_in", "z_in", "dt_in", "conv_x", "conv_b", "conv_c", "rate_in", "bias_in",
    "skip_in", "gain_in", "value_in", "resets", "bucket", "table", "sel_in",
)
OUTPUTS = (
    "o_values", "o_gx", "o_gb", "o_gc", "o_gz", "o_gdt",
)


def scratch_table(T, W, N, H, tn):
    G, C = N // STATE, W // WIDE
    K = C // 2
    per = K // G
    V, D, R = pltpu.VMEM, pltpu.SemaphoreType.DMA, pltpu.SemaphoreType.REGULAR
    return dict(
        x=V((T, W), bf16), b=V((T, N), bf16), c=V((T, N), bf16), z=V((T, W), bf16),
        dt_raw=V((H, T), bf16), wx=V((4, W), f32), wb=V((4, N), f32), wc=V((4, N), f32),
        rate=V((1, H), f32), bias=V((1, H), f32), skip=V((1, H), f32),
        gain=V((1, W), f32), value=V((1, W), f32), rs=V((2, T), jnp.int32),
        xt=V((16, W), bf16), bt=V((16, N), bf16), ct=V((16, N), bf16),
        bk=V((2, T), jnp.int32), tab=V((1, tn), f32),
        vals=V((1, T), f32), gx=V((T, W), bf16), gb=V((T, N), bf16), gc=V((T, N), bf16),
        gz=V((T, W), bf16), gdt=V((H, T), bf16),
        halo_out=V((16, (W + 2 * N) // 4), bf16), halo_in=V((16, (W + 2 * N) // 4), bf16),
        halo_wide=V((16, (W + 2 * N) // 4), f32),
        tail=V((8, W + 2 * N), f32),
        edge_out=V((K, 8, 6 * LANES), f32), edge_in=V((K, 8, 6 * LANES), f32),
        last=V((K, 16, 6 * LANES), f32),
        dec_out=V((8, LANES), f32), dec_in=V((2 * RING, 8, LANES), f32),
        valid=V((3, T, LANES), f32), shifted=V((3, T + 8, LANES), f32),
        mask=V((T, T), f32), start_alive=V((T, LANES), f32), end_alive=V((T, LANES), f32),
        keep=V((16, LANES), f32), target=V((T, LANES), f32),
        pos=V((T + 8, LANES), f32),
        dt=V((T, H), f32), dtp=V((T, H), f32),
        ehl=V((T, 2 * H), bf16), whl=V((T, 2 * H), bf16),
        sel=V((C, 2 * H, WIDE), bf16), rows=V((C, 8, WIDE), f32),
        peer_rows=V((C, 8, WIDE), f32), gw=V((1, W), f32),
        ext=V((2, T + 8, LANES), f32), back=V((2, T + 16, LANES), f32),
        us=V((C, T, WIDE), f32), xc=V((C, T, WIDE), bf16), xs=V((C, 2 * T, WIDE), bf16),
        qg=V((C, 2 * T, WIDE), bf16), yr=V((C, T, WIDE), f32), dy=V((C, T, WIDE), f32),
        ub=V((G, T, STATE), f32), uc=V((G, T, STATE), f32),
        bc=V((G, T, STATE), bf16), cc=V((G, T, STATE), bf16),
        gcr=V((G, T, 2 * T), bf16), gtb=V((G, T, 2 * T), bf16),
        bat=V((G, STATE, T), bf16), crt=V((G, STATE, T), bf16),
        dbs=V((G, T, STATE), f32), dbacc=V((T, STATE), f32),
        sq=V((T, LANES), f32), nu=V((T, LANES), f32),
        vs=V((T, LANES), f32), co=V((T, LANES), f32),
        h1=V((T + 16, 2 * H), f32), h2=V((T, 2 * H), f32), end=V((C, STATE, WIDE), bf16),
        add=V((2, C, STATE, WIDE), bf16), sib_add=V((2, K, STATE, WIDE), bf16),
        chip_add=V((2, K, STATE, WIDE), bf16), chip_start=V((2, K, STATE, WIDE), bf16),
        parts=V((2, RING, K, STATE // RING, WIDE), bf16),
        starts=V((2, RING, K, STATE // RING, WIDE), bf16),
        going=V((2, K, STATE // RING, WIDE), bf16), came=V((2, K, STATE // RING, WIDE), bf16),
        sib_start=V((2, K, STATE, WIDE), bf16),
        in_sem=D((20,)), out_sem=D((7,)), halo_sem=D((2,)), dec_sem=D((2,)),
        edge_sem=D((2,)), sent=D((2, 5)), came_sem=D((2, 5, K)),
    )


def kernel(cn, tn, dims, names, *refs):
    r = dict(zip(list(INPUTS) + list(OUTPUTS) + list(names), refs))

    class Bag:
        pass

    s = Bag()
    for key, ref in r.items():
        setattr(s, key, ref)
    T, W, N, H = dims
    G, C = N // STATE, W // WIDE
    K = C // 2
    per = K // G

    ctx, tp = lax.axis_index("ctx"), lax.axis_index("tp")
    me = lax.rem(ctx, RING)
    square, squares = lax.div(ctx, RING), cn // RING
    sib = {"tp": 1 - tp}
    lower_level, upper_level = square > 0, square < squares - 1

    def member(d):
        return lax.rem(me + d, RING)

    def chip(d):
        return ctx - me + member(d)

    next_block = {"ctx": ctx + tp, "tp": 1 - tp}
    prev_block = {"ctx": ctx - 1 + tp, "tp": 1 - tp}
    has_next = jnp.logical_or(tp == 0, ctx < cn - 1)
    has_prev = jnp.logical_or(tp == 1, ctx > 0)
    cross_next = jnp.logical_and(tp == 1, ctx < cn - 1)
    cross_prev = jnp.logical_and(tp == 0, ctx > 0)

    last_rows = slice(T - 16, T)
    load = {}

    def loader(src, dst, i):
        return lambda: pltpu.make_async_copy(src, dst, s.in_sem.at[i])

    for i, (name, src, dst) in enumerate([
        ("rs", s.resets, s.rs), ("xt", s.x_in.at[last_rows], s.xt),
        ("bt", s.b_in.at[last_rows], s.bt), ("ct", s.c_in.at[last_rows], s.ct),
        ("dt", s.dt_in, s.dt_raw), ("rate", s.rate_in, s.rate), ("bias", s.bias_in, s.bias),
        ("skip", s.skip_in, s.skip), ("sel", s.sel_in, s.sel), ("b", s.b_in, s.b),
        ("c", s.c_in, s.c), ("wb", s.conv_b, s.wb), ("wc", s.conv_c, s.wc), ("x", s.x_in, s.x),
        ("wx", s.conv_x, s.wx), ("z", s.z_in, s.z), ("gain", s.gain_in, s.gain),
        ("value", s.value_in, s.value), ("bk", s.bucket, s.bk), ("tab", s.table, s.tab),
    ]):
        load[name] = loader(src, dst, i)
        load[name]().start()

    def loaded(*which):
        for name in which:
            load[name]().wait()

    barrier = pltpu.get_barrier_semaphore()

    def greet(device):
        pl.semaphore_signal(barrier, inc=1, device_id=device, device_id_type=MESH)

    greet(sib)
    for d in range(1, RING):
        greet({"ctx": chip(d)})
        greet({"ctx": chip(d), "tp": 1 - tp})
    pl.when(upper_level)(lambda: greet({"ctx": ctx + RING}))
    pl.when(lower_level)(lambda: greet({"ctx": ctx - RING}))
    pl.when(cross_next)(lambda: greet(next_block))
    pl.when(cross_prev)(lambda: greet(prev_block))

    def one(flag):
        return jnp.where(flag, 1, 0)

    row_i, col_i = iota((T, T), 0), iota((T, T), 1)
    eye = row_i == col_i
    lower = row_i >= col_i

    def column(row):
        return jnp.sum(jnp.where(eye, row, 0.0), axis=1, keepdims=True)

    loaded("rs")
    real = jnp.broadcast_to(column(s.rs[pl.ds(tp, 1), :].astype(f32)), (T, LANES))
    s.pos[0:8, :] = jnp.zeros((8, LANES), f32)
    s.pos[8 : 8 + T, :] = real
    last_r = s.pos[T + 7 : T + 8, :]
    last_two = jnp.maximum(last_r, s.pos[T + 6 : T + 7, :])
    at = iota((16, LANES), 0)
    keep = jnp.where(at == 13, 1.0 - last_two, jnp.where(at == 14, 1.0 - last_r, 1.0))
    s.keep[...] = keep
    keep8 = keep[8:16, 0:1]

    loaded("xt", "bt", "ct")
    ends = [ref[...].astype(f32)[8:16] * keep8 for ref in (s.xt, s.bt, s.ct)]
    ends = jnp.concatenate(ends, axis=1)
    quarter = (W + 2 * N) // 4
    for q in range(4):
        s.halo_wide[4 * q : 4 * q + 4, :] = ends[4:8, q * quarter : (q + 1) * quarter]
    s.halo_out[...] = s.halo_wide[...].astype(bf16)
    pl.semaphore_wait(
        barrier,
        2 * RING - 1 + one(upper_level) + one(lower_level) + one(cross_next) + one(cross_prev),
    )
    halo = pltpu.make_async_remote_copy(
        src_ref=s.halo_out, dst_ref=s.halo_in, send_sem=s.halo_sem.at[0],
        recv_sem=s.halo_sem.at[1], device_id=next_block, device_id_type=MESH,
    )
    pl.when(has_next)(lambda: halo.start())

    loaded("dt", "rate", "bias", "skip")
    rate, skip = s.rate[...], s.skip[...]
    dtp = s.dt_raw[...].astype(f32).T + s.bias[...]
    dt = jnp.maximum(dtp, 0.0) + jnp.log1p(jnp.exp(-jnp.abs(dtp)))
    s.dtp[...] = dtp
    s.dt[...] = dt
    low = jnp.where(lower, 1.0, 0.0).astype(bf16)
    cum = exact_dot(low, -dt * rate)
    counts = dot(low, real.astype(bf16))
    total = counts[T - 1 : T, :]
    cum_end = cum[T - 1 : T, :]
    eend = jnp.exp(cum_end)
    decay = eend * jnp.where(total[:, :H] == 0.0, 1.0, 0.0)
    s.dec_out[...] = jnp.broadcast_to(twice(decay), (8, 2 * H))

    def tell(d, other):
        return pltpu.make_async_remote_copy(
            src_ref=s.dec_out, dst_ref=s.dec_in.at[2 * me + tp], send_sem=s.dec_sem.at[0],
            recv_sem=s.dec_sem.at[1], device_id={"ctx": chip(d), "tp": lax.rem(tp + other, 2)},
            device_id_type=MESH,
        )

    def all_told():
        ref = s.dec_in.at[0 : 2 * RING - 1]
        return pltpu.make_async_remote_copy(
            src_ref=ref, dst_ref=ref, send_sem=s.dec_sem.at[0], recv_sem=s.dec_sem.at[1],
            device_id=sib, device_id_type=MESH,
        )

    for d in range(RING):
        for other in range(2):
            if d + other > 0:
                tell(d, other).start()
    s.dec_in[2 * me + tp] = s.dec_out[...]

    s.mask[...] = jnp.where(jnp.logical_and(lower, counts == counts.T), 1.0, 0.0)
    s.start_alive[...] = jnp.where(counts == 0.0, 1.0, 0.0)
    s.end_alive[...] = jnp.where(counts == total, 1.0, 0.0)
    one_back, two_back = s.pos[7 : 7 + T, :], s.pos[6 : 6 + T, :]
    second = jnp.maximum(real, one_back)
    for k, flag in enumerate([real, second, jnp.maximum(second, two_back)]):
        s.valid[k] = 1.0 - flag
    for k in range(3):
        m = k + 1
        s.shifted[k, 0:8, :] = jnp.zeros((8, LANES), f32)
        s.shifted[k, T : T + 8, :] = jnp.zeros((8, LANES), f32)
        s.shifted[k, 8 - m : 8 - m + T, :] = s.valid[k]
    for i in range(2):
        s.back[i, 0:8, :] = jnp.zeros((8, LANES), f32)
        s.back[i, T + 8 : T + 16, :] = jnp.zeros((8, LANES), f32)
    s.ehl[...] = jnp.concatenate(two(jnp.exp(cum)), axis=1)
    s.whl[...] = jnp.concatenate(two(jnp.exp(-cum) * dt), axis=1)

    def spread(rows, out):
        halves = jnp.concatenate(two(rows), axis=1)
        for j in range(C):
            out[j] = dot(halves, s.sel[j])

    loaded("sel")
    spread(jnp.concatenate([eend, decay, skip] + [jnp.zeros((1, H), f32)] * 5, axis=0), s.rows)
    loaded("b", "c", "wb", "wc", "x", "wx")

    @pl.when(has_prev)
    def _():
        halo.wait_recv()

    @pl.when(jnp.logical_not(has_prev))
    def _():
        s.halo_in[...] = jnp.zeros(s.halo_in.shape, bf16)

    s.halo_wide[...] = s.halo_in[...].astype(f32)
    for q in range(4):
        s.tail[4:8, q * quarter : (q + 1) * quarter] = s.halo_wide[4 * q : 4 * q + 4, :]

    def conv_pre(slot, piece, tail, w):
        ext = s.ext.at[slot]
        ext[0:8, :] = tail
        ext[8 : 8 + T, :] = piece
        u = w[0:1] * piece
        for k in range(1, 4):
            u = u + (w[k : k + 1] * ext[8 - k : 8 - k + T, :]) * s.valid[k - 1]
        return u

    def conv_back(slot, du, w):
        ext = s.back.at[slot]
        ext[8 : 8 + T, :] = du
        g = w[0:1] * ext[0 : T + 8, :]
        for k in range(1, 4):
            g = g + (w[k : k + 1] * ext[k : k + T + 8, :]) * s.shifted[k - 1]
        return g[0:8], g[8:]

    def silu_both(u):
        sg = sigmoid(u)
        value = u * sg
        return value.astype(bf16), sg + value * (1.0 - sg)

    def lanes(j, i):
        return pl.ds(pl.multiple_of(j * WIDE + i * LANES, LANES), LANES)

    def cols(i):
        return slice(i * LANES, (i + 1) * LANES)

    PART = STATE // RING
    OTHERS = RING - 1

    def rows_of(d):
        return pl.ds(pl.multiple_of(member(d) * PART, PART), PART)

    def ship(way, kind, k, src, dst, device):
        return pltpu.make_async_remote_copy(
            src_ref=src, dst_ref=dst, send_sem=s.sent.at[way, kind],
            recv_sem=s.came_sem.at[way, kind, k], device_id=device, device_id_type=MESH,
        )

    def to_sib(way, k):
        return ship(way, 0, k, s.add.at[way, 2 * k + 1 - tp], s.sib_add.at[way, k], sib)

    def to_owner(way, d, k):
        src, dst = s.chip_add.at[way, k, rows_of(d)], s.parts.at[way, me, k]
        return ship(way, 1, k, src, dst, {"ctx": chip(d)})

    def along(way, k):
        device = {"ctx": ctx + (RING if way == 0 else -RING)}
        return ship(way, 2, k, s.going.at[way, k], s.came.at[way, k], device)

    def from_owner(way, d, k):
        src, dst = s.starts.at[way, member(d), k], s.chip_start.at[way, k, rows_of(0)]
        return ship(way, 3, k, src, dst, {"ctx": chip(d)})

    def arrived(way, kind, k):
        ref = (
            s.sib_add.at[way, k],
            s.parts.at[way, 0:OTHERS, k],
            s.came.at[way, k],
            s.chip_start.at[way, k, 0 : OTHERS * PART],
            s.sib_start.at[way, k],
        )[kind]
        ship(way, kind, k, ref, ref, sib).wait_recv()

    def all_sent(way, kind):
        ref = (
            s.sib_add.at[way],
            s.chip_add.at[way, :, 0 : OTHERS * PART],
            s.going.at[way],
            s.starts.at[way, 0:OTHERS],
            s.sib_start.at[way],
        )[kind]
        ship(way, kind, 0, ref, ref, sib).wait_send()

    def start_ref(way, j):
        return (s.xs if way == 0 else s.qg).at[j, T : 2 * T, :]

    def back_to_sib(way, k):
        return ship(
            way, 4, k, s.sib_start.at[way, k], start_ref(way, 2 * k + tp), sib
        )

    def before(way):
        return lower_level if way == 0 else upper_level

    def after(way):
        return upper_level if way == 0 else lower_level

    def merge_chip(way, k):
        arrived(way, 0, k)
        j = 2 * k + tp
        own, other = s.rows[j, 1:2, :], s.peer_rows[j, RING : RING + 1, :]
        first = tp == way
        ca = jnp.where(first, other, 1.0)
        cb = jnp.where(first, 1.0, own)
        a, b = s.add[way, j].astype(f32), s.sib_add[way, k].astype(f32)
        s.chip_add[way, k] = (ca * a + cb * b).astype(bf16)
        for d in range(1, RING):
            to_owner(way, d, k).start()
        s.parts[way, me, k] = s.chip_add[way, k, rows_of(0), :]

    def merge_square(way, k):
        arrived(way, 1, k)
        pl.when(before(way))(lambda: arrived(way, 2, k))
        state = jnp.where(before(way), s.came[way, k].astype(f32), 0.0)
        decay_rows = s.peer_rows[2 * k + tp]
        for m in range(RING) if way == 0 else range(RING - 1, -1, -1):
            s.starts[way, m, k] = state.astype(bf16)
            state = decay_rows[m : m + 1, :] * state + s.parts[way, m, k].astype(f32)
        s.going[way, k] = state.astype(bf16)
        pl.when(after(way))(lambda: along(way, k).start())
        for d in range(1, RING):
            from_owner(way, d, k).start()
        s.chip_start[way, k, rows_of(0), :] = s.starts[way, me, k]

    def split_chip(way, k):
        arrived(way, 3, k)
        j = 2 * k + tp
        own, other = s.rows[j, 1:2, :], s.peer_rows[j, RING : RING + 1, :]
        t_first = tp == way
        start = s.chip_start[way, k]
        ahead = jnp.where(t_first, s.add[way, j], s.sib_add[way, k]).astype(f32)
        later = (jnp.where(t_first, own, other) * start.astype(f32) + ahead).astype(bf16)
        s.sib_start[way, k] = jnp.where(t_first, later, start)
        back_to_sib(way, k).start()
        start_ref(way, j)[...] = jnp.where(t_first, start, later)

    def start_group(g):
        at_g = pl.ds(pl.multiple_of(g * STATE, STATE), STATE)
        at_b = pl.ds(pl.multiple_of(W + g * STATE, STATE), STATE)
        at_c = pl.ds(pl.multiple_of(W + N + g * STATE, STATE), STATE)
        ub = conv_pre(0, s.b[:, at_g].astype(f32), s.tail[:, at_b], s.wb[:, at_g])
        uc = conv_pre(1, s.c[:, at_g].astype(f32), s.tail[:, at_c], s.wc[:, at_g])
        bb, s.ub[g] = silu_both(ub)
        cb, s.uc[g] = silu_both(uc)
        s.bc[g] = bb
        s.cc[g] = cb
        scores = dot(cb, bb, 1, 1) * s.mask[...]
        ba, cr = bb.astype(f32) * s.end_alive[...], cb.astype(f32) * s.start_alive[...]
        s.gcr[g] = jnp.concatenate([scores, cr], axis=1).astype(bf16)
        s.gtb[g] = jnp.concatenate([scores.T, ba], axis=1).astype(bf16)
        s.bat[g] = ba.T.astype(bf16)
        s.crt[g] = cr.T.astype(bf16)

    def phase_conv(k):
        g = lax.div(k, per)
        pl.when(lax.rem(k, per) == 0)(lambda: start_group(g))
        for jj in range(2):
            j = 2 * k + jj
            weight = dot(s.whl[...], s.sel[j])
            for i in range(2):
                at_x = lanes(j, i)
                u = conv_pre(i, s.x[:, at_x].astype(f32), s.tail[:, at_x], s.wx[:, at_x])
                xc, s.us[j, :, cols(i)] = silu_both(u)
                s.xc[j, :, cols(i)] = xc
                s.xs[j, 0:T, cols(i)] = (xc.astype(f32) * weight[:, cols(i)]).astype(bf16)
            s.add[0, j] = (dot(s.bat[g], s.xs[j, 0:T, :]) * s.rows[j, 0:1, :]).astype(bf16)
        to_sib(0, k).start()

    def run(steps, total):
        def body(i, carry):
            for start, count, step in steps:
                pl.when(jnp.logical_and(i >= start, i < start + count))(
                    partial(step, i - start)
                )
            return carry

        lax.fori_loop(0, total, body, 0)

    def meet_peers(_):
        all_told().wait_recv()
        got = [s.dec_in[i, 0:1, :H] for i in range(2 * RING)]
        chips = [got[2 * m] * got[2 * m + 1] for m in range(RING)]
        other = s.dec_in[2 * me + 1 - tp, 0:1, :H]
        rest = [jnp.zeros((7 - RING, H), f32)]
        spread(jnp.concatenate(chips + [other] + rest, axis=0), s.peer_rows)

    s.sq[...] = jnp.zeros(s.sq.shape, f32)
    s.nu[...] = jnp.zeros(s.nu.shape, f32)

    def prepare_mix(_):
        loaded("z", "gain", "value", "bk", "tab")
        s.gw[...] = s.gain[...] * s.value[...]
        place = column(s.bk[pl.ds(tp, 1), :].astype(f32))
        tabled = jnp.where(place == iota((T, tn), 1).astype(f32), s.tab[...], 0.0)
        s.target[...] = jnp.broadcast_to(jnp.sum(tabled, axis=1, keepdims=True), (T, LANES))

    def phase_mix(k):
        g = lax.div(k, per)
        arrived(0, 4, k)
        for jj in range(2):
            j = 2 * k + jj
            yr = dot(s.gcr[g], s.xs[j])
            s.yr[j] = yr
            carried = s.rows[j, 1:2, :] * s.xs[j, T : 2 * T, :].astype(f32)
            s.end[j] = (s.add[0, j].astype(f32) + carried).astype(bf16)
            reach = dot(s.ehl[...], s.sel[j])
            for i in range(2):
                at_x = lanes(j, i)
                m = reach[:, cols(i)] * yr[:, cols(i)]
                m = m + s.rows[j, 2:3, cols(i)] * s.xc[j, :, cols(i)].astype(f32)
                z = s.z[:, at_x].astype(f32)
                gated = m * (z * sigmoid(z))
                s.sq[...] += gated * gated
                s.nu[...] += gated * s.gw[:, at_x]

    first = F_LAG + F_WAIT * one(before(0))
    run(
        [
            (first, K, partial(merge_square, 0)),
            (first + F_SPLIT, K, partial(split_chip, 0)),
            (0, K, phase_conv),
            (1, 1, meet_peers),
            (1, K, partial(merge_chip, 0)),
            (K, 1, prepare_mix),
            (first + F_MIX, K, phase_mix),
        ],
        F_LAG + F_WAIT + F_MIX + K,
    )

    squares = jnp.sum(s.sq[...], axis=1, keepdims=True)
    numer = jnp.sum(s.nu[...], axis=1, keepdims=True)
    rms = jnp.sqrt(squares / W + epsilon)
    values = numer / rms
    vscale = (values - s.target[...]) / rms
    s.vs[...] = vscale
    s.co[...] = jnp.broadcast_to(values / (rms * W), (T, LANES))
    s.vals[...] = jnp.sum(jnp.where(eye, values, 0.0), axis=0, keepdims=True)

    stores = []

    def store(src, dst, i):
        copy = pltpu.make_async_copy(src, dst, s.out_sem.at[i])
        copy.start()
        stores.append(copy)

    store(s.vals, s.o_values, 0)

    s.h1[...] = jnp.zeros(s.h1.shape, f32)
    s.h2[...] = jnp.zeros(s.h2.shape, f32)

    def head_sums(v, j):
        return dot(v.astype(bf16), s.sel[j], 1, 1)

    def phase_back(k):
        g = lax.div(k, per)
        for jj in range(2):
            j = 2 * k + jj
            reach = dot(s.ehl[...], s.sel[j])
            pieces = []
            for i in range(2):
                at_x = lanes(j, i)
                e, yr = reach[:, cols(i)], s.yr[j, :, cols(i)]
                m = e * yr + s.rows[j, 2:3, cols(i)] * s.xc[j, :, cols(i)].astype(f32)
                z = s.z[:, at_x].astype(f32)
                sg = sigmoid(z)
                gate = z * sg
                gated = m * gate
                dg = s.vs[...] * (s.gw[:, at_x] - s.co[...] * gated)
                s.gz[:, at_x] = (dg * m * (sg + gate * (1.0 - sg))).astype(bf16)
                dy = dg * gate
                s.dy[j, :, cols(i)] = dy
                q = (e * dy).astype(bf16)
                s.qg[j, 0:T, cols(i)] = q
                pieces.append(q.astype(f32) * yr)
            s.h2[...] += head_sums(jnp.concatenate(pieces, axis=1), j)
            s.add[1, j] = dot(s.crt[g], s.qg[j, 0:T, :]).astype(bf16)
        to_sib(1, k).start()

    def edge(at):
        return pltpu.make_async_remote_copy(
            src_ref=s.edge_out.at[at], dst_ref=s.edge_in.at[at], send_sem=s.edge_sem.at[0],
            recv_sem=s.edge_sem.at[1], device_id=prev_block, device_id_type=MESH,
        )

    def gx_part(k):
        at_k = pl.ds(pl.multiple_of(k * 2 * WIDE, 2 * WIDE), 2 * WIDE)
        return pltpu.make_async_copy(
            s.gx.at[0 : T - 16, at_k], s.o_gx.at[0 : T - 16, at_k], s.out_sem.at[6]
        )

    def finish(k, i, slot, du, w, out, at_o):
        head_rows, grad = conv_back(slot, du, w)
        s.edge_out[k, :, cols(i)] = head_rows
        s.last[k, :, cols(i)] = grad[T - 16 :, :]
        out[:, at_o] = grad.astype(bf16)

    def phase_scores(g):
        both = jnp.zeros((T, 2 * T), f32)
        for q in range(2 * per):
            j = 2 * per * g + q
            both = both + dot(s.qg[j, 0:T, :], s.xs[j], 1, 1)
        ds = (both[:, :T] * s.mask[...]).astype(bf16)
        dc = dot(ds, s.bc[g]) + both[:, T:] * s.start_alive[...]
        s.dbs[g] = dot(ds, s.cc[g], 0, 0)
        at_g = pl.ds(pl.multiple_of(g * STATE, STATE), STATE)
        finish(per * g + per - 1, 5, 1, dc * s.uc[g], s.wc[:, at_g], s.gc, at_g)

    def phase_last(k):
        g = lax.div(k, per)
        arrived(1, 4, k)

        @pl.when(lax.rem(k, per) == 0)
        def _():
            s.dbacc[...] = jnp.zeros(s.dbacc.shape, f32)

        for jj in range(2):
            j = 2 * k + jj
            gam = s.qg[j, T : 2 * T, :].astype(f32)
            ends = jnp.sum((gam * s.end[j].astype(f32)).reshape(STATE // 16, 16, WIDE), axis=0)
            ge = (gam * s.rows[j, 0:1, :]).astype(bf16)
            s.qg[j, T : 2 * T, :] = ge
            dxw = dot(s.gtb[g], s.qg[j])
            s.dbacc[...] += dot(s.xs[j, 0:T, :], ge, 1, 1)
            xg = s.xs[j, 0:T, :].astype(f32) * dxw
            s.h1[...] += head_sums(jnp.concatenate([xg, ends], axis=0), j)
            dx = dot(s.whl[...], s.sel[j]) * dxw + s.rows[j, 2:3, :] * s.dy[j]
            for i in range(2):
                at_x = lanes(j, i)
                du = dx[:, cols(i)] * s.us[j, :, cols(i)]
                finish(k, 2 * jj + i, i, du, s.wx[:, at_x], s.gx, at_x)

        @pl.when(lax.rem(k, per) == per - 1)
        def _():
            db = s.dbs[g] + s.dbacc[...] * s.end_alive[...]
            at_g = pl.ds(pl.multiple_of(g * STATE, STATE), STATE)
            finish(k, 4, 0, db * s.ub[g], s.wb[:, at_g], s.gb, at_g)

        pl.when(has_prev)(lambda: edge(k).start())
        gx_part(k).start()

    for k in range(K):
        s.edge_out[k, :, 4 * LANES :] = jnp.zeros((8, 2 * LANES), f32)
        s.last[k, :, 4 * LANES :] = jnp.zeros((16, 2 * LANES), f32)

    def gz_copy():
        return pltpu.make_async_copy(s.gz, s.o_gz, s.out_sem.at[1])

    first = B_LAG + B_WAIT * one(before(1))
    run(
        [
            (first, K, partial(merge_square, 1)),
            (first + B_SPLIT, K, partial(split_chip, 1)),
            (0, K, phase_back),
            (1, K, partial(merge_chip, 1)),
            (K, 1, lambda _: gz_copy().start()),
            (first + B_OUT - B_SCORES * one(before(1)), G, phase_scores),
            (first + B_OUT, K, phase_last),
        ],
        B_LAG + B_WAIT + B_OUT + K,
    )

    h1 = s.h1[0:T, :H]
    dcum = s.h2[:, :H] - h1

    at_end = jnp.sum(s.h1[T : T + 16, :H], axis=0, keepdims=True)
    upper = jnp.where(row_i <= col_i, 1.0, 0.0).astype(bf16)
    ddt = h1 / s.dt[...] - s.rate[...] * (exact_dot(upper, dcum) + at_end)
    s.gdt[...] = (ddt * sigmoid(s.dtp[...])).T.astype(bf16)
    store(s.gdt, s.o_gdt, 2)

    @pl.when(jnp.logical_not(has_next))
    def _():
        s.edge_in[...] = jnp.zeros(s.edge_in.shape, f32)

    pl.when(has_next)(lambda: edge(slice(0, K)).wait_recv())

    def fix(k, carry):
        share = jnp.concatenate([jnp.zeros((8, 6 * LANES), f32), s.edge_in[k]], axis=0)
        fixed = (s.last[k] + share * s.keep[:, 0:1]).astype(bf16)
        at_k = pl.ds(pl.multiple_of(k * 2 * WIDE, 2 * WIDE), 2 * WIDE)
        s.gx[T - 16 : T, at_k] = fixed[:, : 2 * WIDE]

        @pl.when(lax.rem(k, per) == per - 1)
        def _():
            at_g = pl.ds(pl.multiple_of(lax.div(k, per) * STATE, STATE), STATE)
            s.gb[T - 16 : T, at_g] = fixed[:, 2 * WIDE : 2 * WIDE + LANES]
            s.gc[T - 16 : T, at_g] = fixed[:, 2 * WIDE + LANES :]

        return carry

    lax.fori_loop(0, K, fix, 0)
    store(s.gx.at[T - 16 : T, :], s.o_gx.at[T - 16 : T, :], 3)
    store(s.gb, s.o_gb, 4)
    store(s.gc, s.o_gc, 5)

    for way in range(2):
        for kind in (0, 1, 3, 4):
            all_sent(way, kind)
        pl.when(after(way))(partial(all_sent, way, 2))
    pl.when(has_prev)(lambda: edge(slice(0, K)).wait_send())
    all_told().wait_send()
    pltpu.make_async_copy(
        s.gx.at[0 : T - 16], s.o_gx.at[0 : T - 16], s.out_sem.at[6]
    ).wait()
    pl.when(has_next)(lambda: halo.wait_send())
    gz_copy().wait()
    for copy in stores:
        copy.wait()


def pass_on(*refs):
    ins, outs, held, sems = refs[:6], refs[6:12], refs[12:18], refs[18]
    pieces = []
    for i, (a, o, h) in enumerate(zip(ins, outs, held)):
        parts = 4 if a.shape[0] * a.shape[1] > 128 * 1024 else 1
        rows = a.shape[0] // parts
        for q in range(parts):
            at = slice(q * rows, (q + 1) * rows)
            come = pltpu.make_async_copy(a.at[at], h.at[at], sems.at[0, i, q])
            go = pltpu.make_async_copy(h.at[at], o.at[at], sems.at[1, i, q])
            come.start()
            pieces.append((come, go))
    for come, go in pieces:
        come.wait()
        go.start()
    for come, go in pieces:
        go.wait()


def shards(
    x_in, b_in, c_in, z_in, dt_raw, conv_x, conv_b, conv_c, decay_rate, dt_bias, skip_scale,
    norm_gain, w_value, resets, bucket, return_table,
):
    T, W = x_in.shape
    N, H = b_in.shape[1], dt_raw.shape[1]
    tn = return_table.shape[0]
    tpn = lax.axis_size("tp")
    C = W // WIDE
    head = np.arange(2 * H)[None, :, None] % H
    lane_head = np.arange(WIDE)[None, None, :] // HEAD_DIM
    chunk_head = np.arange(C)[:, None, None] * (WIDE // HEAD_DIM)
    sel = jnp.asarray(head == lane_head + chunk_head, bf16)
    args = (
        x_in, b_in, c_in, z_in, dt_raw.T, conv_x, conv_b, conv_c, decay_rate[None, :],
        dt_bias[None, :], skip_scale[None, :], norm_gain[None, :], w_value[None, :],
        resets.reshape(tpn, T), bucket.reshape(tpn, T), return_table[None, :], sel,
    )
    table = scratch_table(T, W, N, H, tn)
    anywhere = pl.BlockSpec(memory_space=pl.ANY)
    outs = pl.pallas_call(
        partial(kernel, lax.axis_size("ctx"), tn, (T, W, N, H), tuple(table)),
        out_shape=[
            jax.ShapeDtypeStruct((1, T), f32), jax.ShapeDtypeStruct((T, W), bf16),
            jax.ShapeDtypeStruct((T, N), bf16), jax.ShapeDtypeStruct((T, N), bf16),
            jax.ShapeDtypeStruct((T, W), bf16), jax.ShapeDtypeStruct((H, T), bf16),
        ],
        in_specs=[anywhere] * len(args),
        out_specs=[anywhere] * 6,
        scratch_shapes=list(table.values()),
        compiler_params=pltpu.CompilerParams(
            collective_id=0, has_side_effects=True, vmem_limit_bytes=58 * 1024 * 1024
        ),
    )(*args)
    values, gx, gb, gc, gz, gdt = pl.pallas_call(
        pass_on,
        out_shape=[jax.ShapeDtypeStruct(o.shape, o.dtype) for o in outs],
        in_specs=[anywhere] * 6,
        out_specs=[anywhere] * 6,
        scratch_shapes=[pltpu.VMEM(o.shape, o.dtype) for o in outs]
        + [pltpu.SemaphoreType.DMA((2, 6, 4))],
    )(*outs)
    return values.reshape(T), gx, gb, gc, gz, gdt.T


def solution(mesh):
    row = P(("group", "ctx", "tp"), None)
    seq = P(("group", "ctx"))
    return jax.shard_map(
        shards,
        mesh=mesh,
        in_specs=(row,) * 5 + (P(),) * 8 + (seq, seq, P()),
        out_specs=(P(("group", "ctx", "tp")),) + (row,) * 5,
        check_vma=False,
    )
```

```python
from functools import partial

import jax
import jax.numpy as jnp
import numpy as np
from jax import lax
from jax.experimental import pallas as pl
from jax.experimental.pallas import tpu as pltpu
from jax.sharding import PartitionSpec as P

HEAD_DIM = 64
STATE = 128
LANES = 128
WIDE = 256
RING = 4
MESH = pl.DeviceIdType.MESH
F_LAG, F_WAIT, F_GIVE, F_SPLIT, F_MIX = 6, 4, 8, 4, 5
B_LAG, B_WAIT, B_GIVE, B_SPLIT, B_OUT, B_SCORES, B_EDGE = 6, 4, 8, 4, 5, 5, 1
EARLY = 4

epsilon = 1e-05
f32 = jnp.float32
bf16 = jnp.bfloat16


def dot(a, b, ca=1, cb=0):
    return lax.dot_general(a, b, (((ca,), (cb,)), ((), ())), preferred_element_type=f32)


def sigmoid(u):
    return 1.0 / (1.0 + jnp.exp(-u))


def iota(shape, dim):
    return lax.broadcasted_iota(jnp.int32, shape, dim)


def two(v):
    high = v.astype(bf16)
    return high, (v - high.astype(f32)).astype(bf16)


def three(v):
    high = v.astype(bf16)
    rest = v - high.astype(f32)
    middle = rest.astype(bf16)
    return high, middle, (rest - middle.astype(f32)).astype(bf16)


def exact_dot(select, v):
    return sum(dot(select, part) for part in three(v))


def twice(v):
    return jnp.concatenate([v, v], axis=1)


INPUTS = (
    "x_in", "b_in", "c_in", "z_in", "dt_in", "conv_x", "conv_b", "conv_c", "rate_in", "bias_in",
    "skip_in", "gain_in", "value_in", "resets", "bucket", "table", "sel_in",
)
OUTPUTS = (
    "o_values", "o_gx", "o_gb", "o_gc", "o_gz", "o_gdt",
)


def scratch_table(T, W, N, H, tn):
    G, C = N // STATE, W // WIDE
    K = C // 2
    per = K // G
    V, D, R = pltpu.VMEM, pltpu.SemaphoreType.DMA, pltpu.SemaphoreType.REGULAR
    return dict(
        x=V((T, W), bf16), b=V((T, N), bf16), c=V((T, N), bf16), z=V((T, W), bf16),
        dt_raw=V((H, T), bf16), wx=V((4, W), f32), wb=V((4, N), f32), wc=V((4, N), f32),
        rate=V((1, H), f32), bias=V((1, H), f32), skip=V((1, H), f32),
        gain=V((1, W), f32), value=V((1, W), f32), rs=V((2, T), jnp.int32),
        xt=V((16, W), bf16), bt=V((16, N), bf16), ct=V((16, N), bf16),
        bk=V((2, T), jnp.int32), tab=V((1, tn), f32),
        vals=V((1, T), f32), gx=V((T, W), bf16), gb=V((T, N), bf16), gc=V((T, N), bf16),
        gz=V((T, W), bf16), gdt=V((H, T), bf16),
        halo_out=V((16, (W + 2 * N) // 4), bf16), halo_in=V((16, (W + 2 * N) // 4), bf16),
        halo_wide=V((16, (W + 2 * N) // 4), f32),
        tail=V((8, W + 2 * N), f32),
        edge_out=V((K, 8, 6 * LANES), f32), edge_in=V((K, 8, 6 * LANES), f32),
        last=V((K, 16, 6 * LANES), f32),
        dec_out=V((8, LANES), f32), dec_in=V((2 * RING, 8, LANES), f32),
        valid=V((3, T, LANES), f32), shifted=V((3, T + 8, LANES), f32),
        mask=V((T, T), f32), start_alive=V((T, LANES), f32), end_alive=V((T, LANES), f32),
        keep=V((16, LANES), f32), target=V((T, LANES), f32),
        pos=V((T + 8, LANES), f32),
        dt=V((T, H), f32), dtp=V((T, H), f32),
        ehl=V((T, 2 * H), bf16), whl=V((T, 2 * H), bf16),
        sel=V((C, 2 * H, WIDE), bf16), rows=V((C, 8, WIDE), f32),
        peer_rows=V((C, 8, WIDE), f32), gw=V((1, W), f32),
        ext=V((4, T + 8, LANES), f32), back=V((4, T + 16, LANES), f32),
        first_rows=V((4, 24, LANES), f32), first_back=V((4, 24, LANES), f32),
        us=V((C, T, WIDE), f32), xc=V((C, T, WIDE), bf16), xs=V((C, 2 * T, WIDE), bf16),
        qg=V((C, 2 * T, WIDE), bf16), yr=V((C, T, WIDE), f32), dy=V((C, T, WIDE), f32),
        ub=V((G, T, STATE), f32), uc=V((G, T, STATE), f32),
        bc=V((G, T, STATE), bf16), cc=V((G, T, STATE), bf16),
        gcr=V((G, T, 2 * T), bf16), gtb=V((G, T, 2 * T), bf16),
        bat=V((G, STATE, T), bf16), crt=V((G, STATE, T), bf16),
        dbs=V((G, T, STATE), f32), dbacc=V((T, STATE), f32),
        sq=V((T, LANES), f32), nu=V((T, LANES), f32),
        vs=V((T, LANES), f32), co=V((T, LANES), f32),
        h1=V((T, 2 * H), f32), h_end=V((16, 2 * H), f32), h2=V((T, 2 * H), f32), end=V((C, STATE, WIDE), bf16),
        add=V((2, C, STATE, WIDE), bf16), sib_add=V((2, K, STATE, WIDE), bf16),
        chip_add=V((2, K, STATE, WIDE), bf16), chip_start=V((2, K, STATE, WIDE), bf16),
        parts=V((2, RING, K, STATE // RING, WIDE), bf16),
        starts=V((2, RING, K, STATE // RING, WIDE), bf16),
        going=V((2, K, STATE // RING, WIDE), bf16), came=V((2, K, STATE // RING, WIDE), bf16),
        sib_start=V((2, K, STATE, WIDE), bf16),
        in_sem=D((20,)), out_sem=D((7,)), halo_sem=D((2,)), dec_sem=D((2,)),
        edge_sem=D((2,)), sent=D((2, 5)), came_sem=D((2, 5, K)),
    )


def kernel(cn, tn, dims, names, *refs):
    r = dict(zip(list(INPUTS) + list(OUTPUTS) + list(names), refs))

    class Bag:
        pass

    s = Bag()
    for key, ref in r.items():
        setattr(s, key, ref)
    T, W, N, H = dims
    G, C = N // STATE, W // WIDE
    K = C // 2
    per = K // G

    ctx, tp = lax.axis_index("ctx"), lax.axis_index("tp")
    me = lax.rem(ctx, RING)
    square, squares = lax.div(ctx, RING), cn // RING
    sib = {"tp": 1 - tp}
    lower_level, upper_level = square > 0, square < squares - 1

    def member(d):
        return lax.rem(me + d, RING)

    def chip(d):
        return ctx - me + member(d)

    next_block = {"ctx": ctx + tp, "tp": 1 - tp}
    prev_block = {"ctx": ctx - 1 + tp, "tp": 1 - tp}
    has_next = jnp.logical_or(tp == 0, ctx < cn - 1)
    has_prev = jnp.logical_or(tp == 1, ctx > 0)
    cross_next = jnp.logical_and(tp == 1, ctx < cn - 1)
    cross_prev = jnp.logical_and(tp == 0, ctx > 0)

    last_rows = slice(T - 16, T)
    load = {}

    def loader(src, dst, i):
        return lambda: pltpu.make_async_copy(src, dst, s.in_sem.at[i])

    for i, (name, src, dst) in enumerate([
        ("rs", s.resets, s.rs), ("xt", s.x_in.at[last_rows], s.xt),
        ("bt", s.b_in.at[last_rows], s.bt), ("ct", s.c_in.at[last_rows], s.ct),
        ("dt", s.dt_in, s.dt_raw), ("rate", s.rate_in, s.rate), ("bias", s.bias_in, s.bias),
        ("skip", s.skip_in, s.skip), ("sel", s.sel_in, s.sel), ("b", s.b_in, s.b),
        ("c", s.c_in, s.c), ("wb", s.conv_b, s.wb), ("wc", s.conv_c, s.wc), ("x", s.x_in, s.x),
        ("wx", s.conv_x, s.wx), ("z", s.z_in, s.z), ("gain", s.gain_in, s.gain),
        ("value", s.value_in, s.value), ("bk", s.bucket, s.bk), ("tab", s.table, s.tab),
    ]):
        load[name] = loader(src, dst, i)
        load[name]().start()

    def loaded(*which):
        for name in which:
            load[name]().wait()

    barrier = pltpu.get_barrier_semaphore()

    def greet(device):
        pl.semaphore_signal(barrier, inc=1, device_id=device, device_id_type=MESH)

    greet(sib)
    for d in range(1, RING):
        greet({"ctx": chip(d)})
        greet({"ctx": chip(d), "tp": 1 - tp})
    pl.when(upper_level)(lambda: greet({"ctx": ctx + RING}))
    pl.when(lower_level)(lambda: greet({"ctx": ctx - RING}))
    pl.when(cross_next)(lambda: greet(next_block))
    pl.when(cross_prev)(lambda: greet(prev_block))

    def one(flag):
        return jnp.where(flag, 1, 0)

    row_i, col_i = iota((T, T), 0), iota((T, T), 1)
    eye = row_i == col_i
    lower = row_i >= col_i

    def column(row):
        return jnp.sum(jnp.where(eye, row, 0.0), axis=1, keepdims=True)

    loaded("rs")
    real = jnp.broadcast_to(column(s.rs[pl.ds(tp, 1), :].astype(f32)), (T, LANES))
    s.pos[0:8, :] = jnp.zeros((8, LANES), f32)
    s.pos[8 : 8 + T, :] = real
    last_r = s.pos[T + 7 : T + 8, :]
    last_two = jnp.maximum(last_r, s.pos[T + 6 : T + 7, :])
    at = iota((16, LANES), 0)
    keep = jnp.where(at == 13, 1.0 - last_two, jnp.where(at == 14, 1.0 - last_r, 1.0))
    s.keep[...] = keep
    keep8 = keep[8:16, 0:1]

    loaded("xt", "bt", "ct")
    ends = [ref[...].astype(f32)[8:16] * keep8 for ref in (s.xt, s.bt, s.ct)]
    ends = jnp.concatenate(ends, axis=1)
    quarter = (W + 2 * N) // 4
    for q in range(4):
        s.halo_wide[4 * q : 4 * q + 4, :] = ends[4:8, q * quarter : (q + 1) * quarter]
    s.halo_out[...] = s.halo_wide[...].astype(bf16)
    loaded("dt", "rate", "bias", "skip")
    rate, skip = s.rate[...], s.skip[...]
    dtp = s.dt_raw[...].astype(f32).T + s.bias[...]
    dt = jnp.maximum(dtp, 0.0) + jnp.log1p(jnp.exp(-jnp.abs(dtp)))
    s.dtp[...] = dtp
    s.dt[...] = dt
    low = jnp.where(lower, 1.0, 0.0).astype(bf16)
    cum = exact_dot(low, -dt * rate)
    counts = dot(low, real.astype(bf16))
    total = counts[T - 1 : T, :]
    cum_end = cum[T - 1 : T, :]
    eend = jnp.exp(cum_end)
    decay = eend * jnp.where(total[:, :H] == 0.0, 1.0, 0.0)
    s.dec_out[...] = jnp.broadcast_to(twice(decay), (8, 2 * H))

    pl.semaphore_wait(
        barrier,
        2 * RING - 1 + one(upper_level) + one(lower_level) + one(cross_next) + one(cross_prev),
    )
    halo = pltpu.make_async_remote_copy(
        src_ref=s.halo_out, dst_ref=s.halo_in, send_sem=s.halo_sem.at[0],
        recv_sem=s.halo_sem.at[1], device_id=next_block, device_id_type=MESH,
    )
    pl.when(has_next)(lambda: halo.start())

    def tell(d, other):
        return pltpu.make_async_remote_copy(
            src_ref=s.dec_out, dst_ref=s.dec_in.at[2 * me + tp], send_sem=s.dec_sem.at[0],
            recv_sem=s.dec_sem.at[1], device_id={"ctx": chip(d), "tp": lax.rem(tp + other, 2)},
            device_id_type=MESH,
        )

    def all_told():
        ref = s.dec_in.at[0 : 2 * RING - 1]
        return pltpu.make_async_remote_copy(
            src_ref=ref, dst_ref=ref, send_sem=s.dec_sem.at[0], recv_sem=s.dec_sem.at[1],
            device_id=sib, device_id_type=MESH,
        )

    for d in range(RING):
        for other in range(2):
            if d + other > 0:
                tell(d, other).start()
    s.dec_in[2 * me + tp] = s.dec_out[...]

    s.mask[...] = jnp.where(jnp.logical_and(lower, counts == counts.T), 1.0, 0.0)
    s.start_alive[...] = jnp.where(counts == 0.0, 1.0, 0.0)
    s.end_alive[...] = jnp.where(counts == total, 1.0, 0.0)
    one_back, two_back = s.pos[7 : 7 + T, :], s.pos[6 : 6 + T, :]
    second = jnp.maximum(real, one_back)
    for k, flag in enumerate([real, second, jnp.maximum(second, two_back)]):
        s.valid[k] = 1.0 - flag
    for k in range(3):
        m = k + 1
        s.shifted[k, 0:8, :] = jnp.zeros((8, LANES), f32)
        s.shifted[k, T : T + 8, :] = jnp.zeros((8, LANES), f32)
        s.shifted[k, 8 - m : 8 - m + T, :] = s.valid[k]
    for i in range(4):
        s.first_back[i, 0:8, :] = jnp.zeros((8, LANES), f32)
        s.back[i, 0:8, :] = jnp.zeros((8, LANES), f32)
        s.back[i, T + 8 : T + 16, :] = jnp.zeros((8, LANES), f32)
    s.ehl[...] = jnp.concatenate(two(jnp.exp(cum)), axis=1)
    s.whl[...] = jnp.concatenate(two(jnp.exp(-cum) * dt), axis=1)

    def spread(rows, out):
        halves = jnp.concatenate(two(rows), axis=1)
        for j in range(C):
            out[j] = dot(halves, s.sel[j])

    loaded("sel")
    spread(jnp.concatenate([eend, decay, skip] + [jnp.zeros((1, H), f32)] * 5, axis=0), s.rows)
    loaded("b", "c", "wb", "wc", "x", "wx")

    def conv_pre(slot, piece, tail, w):
        ext = s.ext.at[slot]
        ext[0:8, :] = tail
        ext[8 : 8 + T, :] = piece
        u = w[0:1] * piece
        for k in range(1, 4):
            u = u + (w[k : k + 1] * ext[8 - k : 8 - k + T, :]) * s.valid[k - 1]
        return u

    def conv_back(slot, du, w):
        ext = s.back.at[slot]
        ext[8 : 8 + T, :] = du
        g = w[0:1] * ext[0 : T + 8, :]
        for k in range(1, 4):
            g = g + (w[k : k + 1] * ext[k : k + T + 8, :]) * s.shifted[k - 1]
        return g[0:8], g[8:]

    def silu_both(u):
        sg = sigmoid(u)
        value = u * sg
        return value.astype(bf16), sg + value * (1.0 - sg)

    def lanes(j, i):
        return pl.ds(pl.multiple_of(j * WIDE + i * LANES, LANES), LANES)

    def cols(i):
        return slice(i * LANES, (i + 1) * LANES)

    PART = STATE // RING
    OTHERS = RING - 1

    def rows_of(d):
        return pl.ds(pl.multiple_of(member(d) * PART, PART), PART)

    def ship(way, kind, k, src, dst, device):
        return pltpu.make_async_remote_copy(
            src_ref=src, dst_ref=dst, send_sem=s.sent.at[way, kind],
            recv_sem=s.came_sem.at[way, kind, k], device_id=device, device_id_type=MESH,
        )

    def to_sib(way, k):
        return ship(way, 0, k, s.add.at[way, 2 * k + 1 - tp], s.sib_add.at[way, k], sib)

    def to_owner(way, d, k):
        src, dst = s.chip_add.at[way, k, rows_of(d)], s.parts.at[way, me, k]
        return ship(way, 1, k, src, dst, {"ctx": chip(d)})

    def along(way, k):
        device = {"ctx": ctx + (RING if way == 0 else -RING)}
        return ship(way, 2, k, s.going.at[way, k], s.came.at[way, k], device)

    def from_owner(way, d, k):
        src, dst = s.starts.at[way, member(d), k], s.chip_start.at[way, k, rows_of(0)]
        return ship(way, 3, k, src, dst, {"ctx": chip(d)})

    def arrived(way, kind, k):
        ref = (
            s.sib_add.at[way, k],
            s.parts.at[way, 0:OTHERS, k],
            s.came.at[way, k],
            s.chip_start.at[way, k, 0 : OTHERS * PART],
            s.sib_start.at[way, k],
        )[kind]
        ship(way, kind, k, ref, ref, sib).wait_recv()

    def all_sent(way, kind):
        ref = (
            s.sib_add.at[way],
            s.chip_add.at[way, :, 0 : OTHERS * PART],
            s.going.at[way],
            s.starts.at[way, 0:OTHERS],
            s.sib_start.at[way],
        )[kind]
        ship(way, kind, 0, ref, ref, sib).wait_send()

    def start_ref(way, j):
        return (s.xs if way == 0 else s.qg).at[j, T : 2 * T, :]

    def back_to_sib(way, k):
        return ship(
            way, 4, k, s.sib_start.at[way, k], start_ref(way, 2 * k + tp), sib
        )

    def before(way):
        return lower_level if way == 0 else upper_level

    def after(way):
        return upper_level if way == 0 else lower_level

    def merge_chip(way, k):
        arrived(way, 0, k)
        j = 2 * k + tp
        own, other = s.rows[j, 1:2, :], s.peer_rows[j, RING : RING + 1, :]
        first = tp == way
        ca = jnp.where(first, other, 1.0)
        cb = jnp.where(first, 1.0, own)
        a, b = s.add[way, j].astype(f32), s.sib_add[way, k].astype(f32)
        s.chip_add[way, k] = (ca * a + cb * b).astype(bf16)
        for d in range(1, RING):
            to_owner(way, d, k).start()
        s.parts[way, me, k] = s.chip_add[way, k, rows_of(0), :]

    def merge_square(way, k):
        arrived(way, 1, k)
        pl.when(before(way))(lambda: arrived(way, 2, k))
        state = jnp.where(before(way), s.came[way, k].astype(f32), 0.0)
        decay_rows = s.peer_rows[2 * k + tp]
        for m in range(RING) if way == 0 else range(RING - 1, -1, -1):
            s.starts[way, m, k] = state.astype(bf16)
            state = decay_rows[m : m + 1, :] * state + s.parts[way, m, k].astype(f32)
        s.going[way, k] = state.astype(bf16)
        pl.when(after(way))(lambda: along(way, k).start())
        s.chip_start[way, k, rows_of(0), :] = s.starts[way, me, k]

    def give(way, k):
        for d in range(1, RING):
            from_owner(way, d, k).start()

    def split_chip(way, k):
        arrived(way, 3, k)
        j = 2 * k + tp
        own, other = s.rows[j, 1:2, :], s.peer_rows[j, RING : RING + 1, :]
        t_first = tp == way
        start = s.chip_start[way, k]
        ahead = jnp.where(t_first, s.add[way, j], s.sib_add[way, k]).astype(f32)
        later = (jnp.where(t_first, own, other) * start.astype(f32) + ahead).astype(bf16)
        s.sib_start[way, k] = jnp.where(t_first, later, start)
        back_to_sib(way, k).start()
        start_ref(way, j)[...] = jnp.where(t_first, start, later)

    def start_group(g):
        at_g = pl.ds(pl.multiple_of(g * STATE, STATE), STATE)
        at_b = pl.ds(pl.multiple_of(W + g * STATE, STATE), STATE)
        at_c = pl.ds(pl.multiple_of(W + N + g * STATE, STATE), STATE)
        ub = conv_pre(0, s.b[:, at_g].astype(f32), s.tail[:, at_b], s.wb[:, at_g])
        uc = conv_pre(1, s.c[:, at_g].astype(f32), s.tail[:, at_c], s.wc[:, at_g])
        bb, s.ub[g] = silu_both(ub)
        cb, s.uc[g] = silu_both(uc)
        s.bc[g] = bb
        s.cc[g] = cb
        scores = dot(cb, bb, 1, 1) * s.mask[...]
        ba, cr = bb.astype(f32) * s.end_alive[...], cb.astype(f32) * s.start_alive[...]
        s.gcr[g] = jnp.concatenate([scores, cr], axis=1).astype(bf16)
        s.gtb[g] = jnp.concatenate([scores.T, ba], axis=1).astype(bf16)
        s.bat[g] = ba.T.astype(bf16)
        s.crt[g] = cr.T.astype(bf16)

    def conv_first(k, carry=None):
        for jj in range(2):
            j = 2 * k + jj
            weight = dot(s.whl[...], s.sel[j])
            for i in range(2):
                at_x = lanes(j, i)
                none = jnp.zeros((8, LANES), f32)
                u = conv_pre(2 * jj + i, s.x[:, at_x].astype(f32), none, s.wx[:, at_x])
                xc, s.us[j, :, cols(i)] = silu_both(u)
                s.xc[j, :, cols(i)] = xc
                s.xs[j, 0:T, cols(i)] = (xc.astype(f32) * weight[:, cols(i)]).astype(bf16)
        return carry

    def phase_conv(k):
        g = lax.div(k, per)
        pl.when(lax.rem(k, per) == 0)(lambda: start_group(g))
        for jj in range(2):
            j = 2 * k + jj
            weight = dot(s.whl[0:16, :], s.sel[j])
            for i in range(2):
                at_x = lanes(j, i)
                ext = s.first_rows.at[2 * jj + i]
                piece = s.x[0:16, at_x].astype(f32)
                ext[0:8, :] = s.tail[:, at_x]
                ext[8:24, :] = piece
                w = s.wx[:, at_x]
                u = w[0:1] * piece
                for m in range(1, 4):
                    u = u + (w[m : m + 1] * ext[8 - m : 24 - m, :]) * s.valid[m - 1, 0:16, :]
                xc, s.us[j, 0:16, cols(i)] = silu_both(u)
                s.xc[j, 0:16, cols(i)] = xc
                s.xs[j, 0:16, cols(i)] = (xc.astype(f32) * weight[:, cols(i)]).astype(bf16)
            s.add[0, j] = (dot(s.bat[g], s.xs[j, 0:T, :]) * s.rows[j, 0:1, :]).astype(bf16)
        to_sib(0, k).start()

    lax.fori_loop(0, EARLY, conv_first, None)

    @pl.when(has_prev)
    def _():
        halo.wait_recv()

    @pl.when(jnp.logical_not(has_prev))
    def _():
        s.halo_in[...] = jnp.zeros(s.halo_in.shape, bf16)

    s.halo_wide[...] = s.halo_in[...].astype(f32)
    for q in range(4):
        s.tail[4:8, q * quarter : (q + 1) * quarter] = s.halo_wide[4 * q : 4 * q + 4, :]

    def run(steps, total):
        def body(i, carry):
            for start, count, step in steps:
                pl.when(jnp.logical_and(i >= start, i < start + count))(
                    partial(step, i - start)
                )
            return carry

        lax.fori_loop(0, total, body, 0)

    def meet_peers(_):
        all_told().wait_recv()
        got = [s.dec_in[i, 0:1, :H] for i in range(2 * RING)]
        chips = [got[2 * m] * got[2 * m + 1] for m in range(RING)]
        other = s.dec_in[2 * me + 1 - tp, 0:1, :H]
        rest = [jnp.zeros((7 - RING, H), f32)]
        spread(jnp.concatenate(chips + [other] + rest, axis=0), s.peer_rows)

    s.sq[...] = jnp.zeros(s.sq.shape, f32)
    s.nu[...] = jnp.zeros(s.nu.shape, f32)

    def prepare_mix(_):
        loaded("z", "gain", "value", "bk", "tab")
        s.gw[...] = s.gain[...] * s.value[...]
        place = column(s.bk[pl.ds(tp, 1), :].astype(f32))
        tabled = jnp.where(place == iota((T, tn), 1).astype(f32), s.tab[...], 0.0)
        s.target[...] = jnp.broadcast_to(jnp.sum(tabled, axis=1, keepdims=True), (T, LANES))

    def phase_mix(k):
        g = lax.div(k, per)
        arrived(0, 4, k)
        for jj in range(2):
            j = 2 * k + jj
            yr = dot(s.gcr[g], s.xs[j])
            s.yr[j] = yr
            carried = s.rows[j, 1:2, :] * s.xs[j, T : 2 * T, :].astype(f32)
            s.end[j] = (s.add[0, j].astype(f32) + carried).astype(bf16)
            reach = dot(s.ehl[...], s.sel[j])
            for i in range(2):
                at_x = lanes(j, i)
                m = reach[:, cols(i)] * yr[:, cols(i)]
                m = m + s.rows[j, 2:3, cols(i)] * s.xc[j, :, cols(i)].astype(f32)
                z = s.z[:, at_x].astype(f32)
                gated = m * (z * sigmoid(z))
                s.sq[...] += gated * gated
                s.nu[...] += gated * s.gw[:, at_x]

    first = F_LAG + F_WAIT * one(before(0))
    given = first + F_GIVE * one(after(0))
    run(
        [
            (first, K, partial(merge_square, 0)),
            (given, K, partial(give, 0)),
            (given + F_SPLIT, K, partial(split_chip, 0)),
            (0, K, phase_conv),
            (0, K - EARLY, lambda k: conv_first(k + EARLY)),
            (1, 1, meet_peers),
            (1, K, partial(merge_chip, 0)),
            (K, 1, prepare_mix),
            (given + F_MIX, K, phase_mix),
        ],
        F_LAG + F_WAIT + F_GIVE + F_MIX + K,
    )

    squares = jnp.sum(s.sq[...], axis=1, keepdims=True)
    numer = jnp.sum(s.nu[...], axis=1, keepdims=True)
    rms = jnp.sqrt(squares / W + epsilon)
    values = numer / rms
    vscale = (values - s.target[...]) / rms
    s.vs[...] = vscale
    s.co[...] = jnp.broadcast_to(values / (rms * W), (T, LANES))
    s.vals[...] = jnp.sum(jnp.where(eye, values, 0.0), axis=0, keepdims=True)

    stores = []

    def store(src, dst, i):
        copy = pltpu.make_async_copy(src, dst, s.out_sem.at[i])
        copy.start()
        stores.append(copy)

    store(s.vals, s.o_values, 0)

    s.h1[...] = jnp.zeros(s.h1.shape, f32)
    s.h_end[...] = jnp.zeros(s.h_end.shape, f32)
    s.h2[...] = jnp.zeros(s.h2.shape, f32)

    def head_sums(v, j):
        return dot(v.astype(bf16), s.sel[j], 1, 1)

    def phase_back(k):
        g = lax.div(k, per)
        for jj in range(2):
            j = 2 * k + jj
            reach = dot(s.ehl[...], s.sel[j])
            pieces = []
            for i in range(2):
                at_x = lanes(j, i)
                e, yr = reach[:, cols(i)], s.yr[j, :, cols(i)]
                m = e * yr + s.rows[j, 2:3, cols(i)] * s.xc[j, :, cols(i)].astype(f32)
                z = s.z[:, at_x].astype(f32)
                sg = sigmoid(z)
                gate = z * sg
                gated = m * gate
                dg = s.vs[...] * (s.gw[:, at_x] - s.co[...] * gated)
                s.gz[:, at_x] = (dg * m * (sg + gate * (1.0 - sg))).astype(bf16)
                dy = dg * gate
                s.dy[j, :, cols(i)] = dy
                q = (e * dy).astype(bf16)
                s.qg[j, 0:T, cols(i)] = q
                pieces.append(q.astype(f32) * yr)
            s.h2[...] += head_sums(jnp.concatenate(pieces, axis=1), j)
            s.add[1, j] = dot(s.crt[g], s.qg[j, 0:T, :]).astype(bf16)
        to_sib(1, k).start()

    def edge(at):
        return pltpu.make_async_remote_copy(
            src_ref=s.edge_out.at[at], dst_ref=s.edge_in.at[at], send_sem=s.edge_sem.at[0],
            recv_sem=s.edge_sem.at[1], device_id=prev_block, device_id_type=MESH,
        )

    def gx_part(k):
        at_k = pl.ds(pl.multiple_of(k * 2 * WIDE, 2 * WIDE), 2 * WIDE)
        return pltpu.make_async_copy(
            s.gx.at[0 : T - 16, at_k], s.o_gx.at[0 : T - 16, at_k], s.out_sem.at[6]
        )

    def finish(k, i, slot, du, w, out, at_o):
        head_rows, grad = conv_back(slot, du, w)
        s.last[k, :, cols(i)] = grad[T - 16 :, :]
        out[:, at_o] = grad.astype(bf16)
        return head_rows

    def finish_edge(k, i, *rest):
        s.edge_out[k, :, cols(i)] = finish(k, i, *rest)

    def phase_scores(g):
        both = jnp.zeros((T, 2 * T), f32)
        for q in range(2 * per):
            j = 2 * per * g + q
            both = both + dot(s.qg[j, 0:T, :], s.xs[j], 1, 1)
        ds = (both[:, :T] * s.mask[...]).astype(bf16)
        dc = dot(ds, s.bc[g]) + both[:, T:] * s.start_alive[...]
        s.dbs[g] = dot(ds, s.cc[g], 0, 0)
        at_g = pl.ds(pl.multiple_of(g * STATE, STATE), STATE)
        finish_edge(per * g + per - 1, 5, 1, dc * s.uc[g], s.wc[:, at_g], s.gc, at_g)

    def phase_edge(k):
        g = lax.div(k, per)
        arrived(1, 4, k)

        @pl.when(lax.rem(k, per) == 0)
        def _():
            s.dbacc[...] = jnp.zeros(s.dbacc.shape, f32)

        db, h_end = 0.0, 0.0
        for jj in range(2):
            j = 2 * k + jj
            gam = s.qg[j, T : 2 * T, :].astype(f32)
            ends = jnp.sum((gam * s.end[j].astype(f32)).reshape(STATE // 16, 16, WIDE), axis=0)
            h_end = h_end + head_sums(ends, j)
            ge = (gam * s.rows[j, 0:1, :]).astype(bf16)
            s.qg[j, T : 2 * T, :] = ge
            db = db + dot(s.xs[j, 0:T, :], ge, 1, 1)
            dxw = dot(s.gtb[g, 0:16, 0:T], s.qg[j, 0:T, :]) + dot(s.gtb[g, 0:16, T:], ge)
            dx = dot(s.whl[0:16, :], s.sel[j]) * dxw + s.rows[j, 2:3, :] * s.dy[j, 0:16, :]
            for i in range(2):
                ext = s.first_back.at[2 * jj + i]
                ext[8:24, :] = dx[:, cols(i)] * s.us[j, 0:16, cols(i)]
                w = s.wx[:, lanes(j, i)]
                rows = 0.0
                for m in range(1, 4):
                    rows = rows + (w[m : m + 1] * ext[m : m + 8, :]) * s.shifted[m - 1, 0:8, :]
                s.edge_out[k, :, cols(2 * jj + i)] = rows
        s.h_end[...] += h_end
        s.dbacc[...] += db

        @pl.when(lax.rem(k, per) == per - 1)
        def _():
            grad_b = s.dbs[g] + s.dbacc[...] * s.end_alive[...]
            at_g = pl.ds(pl.multiple_of(g * STATE, STATE), STATE)
            finish_edge(k, 4, 0, grad_b * s.ub[g], s.wb[:, at_g], s.gb, at_g)

        pl.when(has_prev)(lambda: edge(k).start())

    def phase_last(k):
        g = lax.div(k, per)
        h1 = 0.0
        for jj in range(2):
            j = 2 * k + jj
            dxw = dot(s.gtb[g], s.qg[j])
            h1 = h1 + head_sums(s.xs[j, 0:T, :].astype(f32) * dxw, j)
            dx = dot(s.whl[...], s.sel[j]) * dxw + s.rows[j, 2:3, :] * s.dy[j]
            for i in range(2):
                at_x = lanes(j, i)
                du = dx[:, cols(i)] * s.us[j, :, cols(i)]
                finish(k, 2 * jj + i, 2 * jj + i, du, s.wx[:, at_x], s.gx, at_x)
        s.h1[...] += h1
        gx_part(k).start()

    for k in range(K):
        s.edge_out[k, :, 4 * LANES :] = jnp.zeros((8, 2 * LANES), f32)
        s.last[k, :, 4 * LANES :] = jnp.zeros((16, 2 * LANES), f32)

    def gz_copy():
        return pltpu.make_async_copy(s.gz, s.o_gz, s.out_sem.at[1])

    first = B_LAG + B_WAIT * one(before(1))
    given = first + B_GIVE * one(after(1))
    run(
        [
            (first, K, partial(merge_square, 1)),
            (given, K, partial(give, 1)),
            (given + B_SPLIT, K, partial(split_chip, 1)),
            (0, K, phase_back),
            (1, K, partial(merge_chip, 1)),
            (K, 1, lambda _: gz_copy().start()),
            (given + B_OUT - B_SCORES, G, phase_scores),
            (given + B_OUT, K, phase_edge),
            (given + B_OUT + B_EDGE, K, phase_last),
        ],
        B_LAG + B_WAIT + B_GIVE + B_OUT + B_EDGE + K,
    )

    h1 = s.h1[:, :H]
    dcum = s.h2[:, :H] - h1

    at_end = jnp.sum(s.h_end[:, :H], axis=0, keepdims=True)
    upper = jnp.where(row_i <= col_i, 1.0, 0.0).astype(bf16)
    ddt = h1 / s.dt[...] - s.rate[...] * (exact_dot(upper, dcum) + at_end)
    s.gdt[...] = (ddt * sigmoid(s.dtp[...])).T.astype(bf16)
    store(s.gdt, s.o_gdt, 2)

    @pl.when(jnp.logical_not(has_next))
    def _():
        s.edge_in[...] = jnp.zeros(s.edge_in.shape, f32)

    pl.when(has_next)(lambda: edge(slice(0, K)).wait_recv())

    def fix(k, carry):
        share = jnp.concatenate([jnp.zeros((8, 6 * LANES), f32), s.edge_in[k]], axis=0)
        fixed = (s.last[k] + share * s.keep[:, 0:1]).astype(bf16)
        at_k = pl.ds(pl.multiple_of(k * 2 * WIDE, 2 * WIDE), 2 * WIDE)
        s.gx[T - 16 : T, at_k] = fixed[:, : 2 * WIDE]

        @pl.when(lax.rem(k, per) == per - 1)
        def _():
            at_g = pl.ds(pl.multiple_of(lax.div(k, per) * STATE, STATE), STATE)
            s.gb[T - 16 : T, at_g] = fixed[:, 2 * WIDE : 2 * WIDE + LANES]
            s.gc[T - 16 : T, at_g] = fixed[:, 2 * WIDE + LANES :]

        return carry

    lax.fori_loop(0, K, fix, 0)
    store(s.gx.at[T - 16 : T, :], s.o_gx.at[T - 16 : T, :], 3)
    store(s.gb, s.o_gb, 4)
    store(s.gc, s.o_gc, 5)

    for way in range(2):
        for kind in (0, 1, 3, 4):
            all_sent(way, kind)
        pl.when(after(way))(partial(all_sent, way, 2))
    pl.when(has_prev)(lambda: edge(slice(0, K)).wait_send())
    all_told().wait_send()
    pltpu.make_async_copy(
        s.gx.at[0 : T - 16], s.o_gx.at[0 : T - 16], s.out_sem.at[6]
    ).wait()
    pl.when(has_next)(lambda: halo.wait_send())
    gz_copy().wait()
    for copy in stores:
        copy.wait()


def pass_on(*refs):
    ins, outs, held, sems = refs[:6], refs[6:12], refs[12:18], refs[18]
    pieces = []
    for i, (a, o, h) in enumerate(zip(ins, outs, held)):
        parts = 4 if a.shape[0] * a.shape[1] > 128 * 1024 else 1
        rows = a.shape[0] // parts
        for q in range(parts):
            at = slice(q * rows, (q + 1) * rows)
            come = pltpu.make_async_copy(a.at[at], h.at[at], sems.at[0, i, q])
            go = pltpu.make_async_copy(h.at[at], o.at[at], sems.at[1, i, q])
            come.start()
            pieces.append((come, go))
    for come, go in pieces:
        come.wait()
        go.start()
    for come, go in pieces:
        go.wait()


def shards(
    x_in, b_in, c_in, z_in, dt_raw, conv_x, conv_b, conv_c, decay_rate, dt_bias, skip_scale,
    norm_gain, w_value, resets, bucket, return_table,
):
    T, W = x_in.shape
    N, H = b_in.shape[1], dt_raw.shape[1]
    tn = return_table.shape[0]
    tpn = lax.axis_size("tp")
    C = W // WIDE
    head = np.arange(2 * H)[None, :, None] % H
    lane_head = np.arange(WIDE)[None, None, :] // HEAD_DIM
    chunk_head = np.arange(C)[:, None, None] * (WIDE // HEAD_DIM)
    sel = jnp.asarray(head == lane_head + chunk_head, bf16)
    args = (
        x_in, b_in, c_in, z_in, dt_raw.T, conv_x, conv_b, conv_c, decay_rate[None, :],
        dt_bias[None, :], skip_scale[None, :], norm_gain[None, :], w_value[None, :],
        resets.reshape(tpn, T), bucket.reshape(tpn, T), return_table[None, :], sel,
    )
    table = scratch_table(T, W, N, H, tn)
    anywhere = pl.BlockSpec(memory_space=pl.ANY)
    outs = pl.pallas_call(
        partial(kernel, lax.axis_size("ctx"), tn, (T, W, N, H), tuple(table)),
        out_shape=[
            jax.ShapeDtypeStruct((1, T), f32), jax.ShapeDtypeStruct((T, W), bf16),
            jax.ShapeDtypeStruct((T, N), bf16), jax.ShapeDtypeStruct((T, N), bf16),
            jax.ShapeDtypeStruct((T, W), bf16), jax.ShapeDtypeStruct((H, T), bf16),
        ],
        in_specs=[anywhere] * len(args),
        out_specs=[anywhere] * 6,
        scratch_shapes=list(table.values()),
        compiler_params=pltpu.CompilerParams(
            collective_id=0, has_side_effects=True, vmem_limit_bytes=58 * 1024 * 1024
        ),
    )(*args)
    values, gx, gb, gc, gz, gdt = pl.pallas_call(
        pass_on,
        out_shape=[jax.ShapeDtypeStruct(o.shape, o.dtype) for o in outs],
        in_specs=[anywhere] * 6,
        out_specs=[anywhere] * 6,
        scratch_shapes=[pltpu.VMEM(o.shape, o.dtype) for o in outs]
        + [pltpu.SemaphoreType.DMA((2, 6, 4))],
    )(*outs)
    return values.reshape(T), gx, gb, gc, gz, gdt.T


def solution(mesh):
    row = P(("group", "ctx", "tp"), None)
    seq = P(("group", "ctx"))
    return jax.shard_map(
        shards,
        mesh=mesh,
        in_specs=(row,) * 5 + (P(),) * 8 + (seq, seq, P()),
        out_specs=(P(("group", "ctx", "tp")),) + (row,) * 5,
        check_vma=False,
    )
```

```python
from functools import partial

import jax
import jax.numpy as jnp
import numpy as np
from jax import lax
from jax.experimental import pallas as pl
from jax.experimental.pallas import tpu as pltpu
from jax.sharding import PartitionSpec as P

HEAD_DIM = 64
STATE = 128
LANES = 128
WIDE = 256
RING = 4
MESH = pl.DeviceIdType.MESH
F_LAG, F_WAIT, F_GIVE, F_SPLIT, F_MIX = 6, 4, 6, 4, 5
B_LAG, B_WAIT, B_GIVE, B_SPLIT, B_OUT, B_SCORES, B_EDGE = 6, 4, 6, 4, 5, 5, 1
EARLY = 4

epsilon = 1e-05
f32 = jnp.float32
bf16 = jnp.bfloat16


def dot(a, b, ca=1, cb=0):
    return lax.dot_general(a, b, (((ca,), (cb,)), ((), ())), preferred_element_type=f32)


def sigmoid(u):
    return 1.0 / (1.0 + jnp.exp(-u))


def iota(shape, dim):
    return lax.broadcasted_iota(jnp.int32, shape, dim)


def two(v):
    high = v.astype(bf16)
    return high, (v - high.astype(f32)).astype(bf16)


def three(v):
    high = v.astype(bf16)
    rest = v - high.astype(f32)
    middle = rest.astype(bf16)
    return high, middle, (rest - middle.astype(f32)).astype(bf16)


def exact_dot(select, v):
    return sum(dot(select, part) for part in three(v))


def twice(v):
    return jnp.concatenate([v, v], axis=1)


INPUTS = (
    "x_in", "b_in", "c_in", "z_in", "dt_in", "conv_x", "conv_b", "conv_c", "rate_in", "bias_in",
    "skip_in", "gain_in", "value_in", "resets", "bucket", "table", "sel_in",
)
OUTPUTS = (
    "o_values", "o_gx", "o_gb", "o_gc", "o_gz", "o_gdt",
)


def scratch_table(T, W, N, H, tn):
    G, C = N // STATE, W // WIDE
    K = C // 2
    per = K // G
    V, D, R = pltpu.VMEM, pltpu.SemaphoreType.DMA, pltpu.SemaphoreType.REGULAR
    return dict(
        x=V((T, W), bf16), b=V((T, N), bf16), c=V((T, N), bf16), z=V((T, W), bf16),
        dt_raw=V((H, T), bf16), wx=V((4, W), f32), wb=V((4, N), f32), wc=V((4, N), f32),
        rate=V((1, H), f32), bias=V((1, H), f32), skip=V((1, H), f32),
        gain=V((1, W), f32), value=V((1, W), f32), rs=V((2, T), jnp.int32),
        xt=V((16, W), bf16), bt=V((16, N), bf16), ct=V((16, N), bf16),
        bk=V((2, T), jnp.int32), tab=V((1, tn), f32),
        vals=V((1, T), f32), gx=V((T, W), bf16), gb=V((T, N), bf16), gc=V((T, N), bf16),
        gz=V((T, W), bf16), gdt=V((H, T), bf16),
        halo_out=V((16, (W + 2 * N) // 4), bf16), halo_in=V((16, (W + 2 * N) // 4), bf16),
        halo_wide=V((16, (W + 2 * N) // 4), f32),
        tail=V((8, W + 2 * N), f32),
        edge_out=V((K, 4, 6 * LANES), f32), edge_in=V((K, 4, 6 * LANES), f32),
        last=V((K, 16, 6 * LANES), f32),
        dec_out=V((8, LANES), f32), dec_in=V((2 * RING, 8, LANES), f32),
        valid=V((3, T, LANES), f32), shifted=V((3, T + 8, LANES), f32),
        mask=V((T, T), f32), start_alive=V((T, LANES), f32), end_alive=V((T, LANES), f32),
        keep=V((16, LANES), f32), target=V((T, LANES), f32),
        pos=V((T + 8, LANES), f32),
        dt=V((T, H), f32), dtp=V((T, H), f32),
        ehl=V((T, 2 * H), bf16), whl=V((T, 2 * H), bf16),
        sel=V((C, 2 * H, WIDE), bf16), rows=V((C, 8, WIDE), f32),
        peer_rows=V((C, 8, WIDE), f32), gw=V((1, W), f32),
        ext=V((4, T + 8, LANES), f32), back=V((4, T + 16, LANES), f32),
        first_rows=V((4, 24, LANES), f32), first_back=V((4, 24, LANES), f32),
        us=V((C, T, WIDE), f32), xc=V((C, T, WIDE), bf16), xs=V((C, 2 * T, WIDE), bf16),
        qg=V((C, 2 * T, WIDE), bf16), yr=V((C, T, WIDE), f32), dy=V((C, T, WIDE), f32),
        ub=V((G, T, STATE), f32), uc=V((G, T, STATE), f32),
        bc=V((G, T, STATE), bf16), cc=V((G, T, STATE), bf16),
        gcr=V((G, T, 2 * T), bf16), gtb=V((G, T, 2 * T), bf16),
        bat=V((G, STATE, T), bf16), crt=V((G, STATE, T), bf16),
        dbs=V((G, T, STATE), f32), dbacc=V((T, STATE), f32),
        sq=V((T, LANES), f32), nu=V((T, LANES), f32),
        vs=V((T, LANES), f32), co=V((T, LANES), f32),
        h1=V((T, 2 * H), f32), h_end=V((16, 2 * H), f32), h2=V((T, 2 * H), f32), end=V((C, STATE, WIDE), bf16),
        add=V((2, C, STATE, WIDE), bf16), sib_add=V((2, K, STATE, WIDE), bf16),
        chip_add=V((2, K, STATE, WIDE), bf16), chip_start=V((2, K, STATE, WIDE), bf16),
        parts=V((2, RING, K, STATE // RING, WIDE), bf16),
        starts=V((2, RING, K, STATE // RING, WIDE), bf16),
        going=V((2, K, STATE // RING, WIDE), bf16), came=V((2, K, STATE // RING, WIDE), bf16),
        sib_start=V((2, K, STATE, WIDE), bf16),
        in_sem=D((20,)), out_sem=D((7,)), halo_sem=D((2,)), dec_sem=D((2,)),
        edge_sem=D((2,)), sent=D((2, 5)), came_sem=D((2, 5, K)),
    )


def kernel(cn, tn, dims, names, *refs):
    r = dict(zip(list(INPUTS) + list(OUTPUTS) + list(names), refs))

    class Bag:
        pass

    s = Bag()
    for key, ref in r.items():
        setattr(s, key, ref)
    T, W, N, H = dims
    G, C = N // STATE, W // WIDE
    K = C // 2
    per = K // G

    ctx, tp = lax.axis_index("ctx"), lax.axis_index("tp")
    me = lax.rem(ctx, RING)
    square, squares = lax.div(ctx, RING), cn // RING
    sib = {"tp": 1 - tp}
    lower_level, upper_level = square > 0, square < squares - 1

    def member(d):
        return lax.rem(me + d, RING)

    def chip(d):
        return ctx - me + member(d)

    next_block = {"ctx": ctx + tp, "tp": 1 - tp}
    prev_block = {"ctx": ctx - 1 + tp, "tp": 1 - tp}
    has_next = jnp.logical_or(tp == 0, ctx < cn - 1)
    has_prev = jnp.logical_or(tp == 1, ctx > 0)
    cross_next = jnp.logical_and(tp == 1, ctx < cn - 1)
    cross_prev = jnp.logical_and(tp == 0, ctx > 0)

    last_rows = slice(T - 16, T)
    load = {}

    def loader(src, dst, i):
        return lambda: pltpu.make_async_copy(src, dst, s.in_sem.at[i])

    for i, (name, src, dst) in enumerate([
        ("rs", s.resets, s.rs), ("xt", s.x_in.at[last_rows], s.xt),
        ("bt", s.b_in.at[last_rows], s.bt), ("ct", s.c_in.at[last_rows], s.ct),
        ("dt", s.dt_in, s.dt_raw), ("rate", s.rate_in, s.rate), ("bias", s.bias_in, s.bias),
        ("skip", s.skip_in, s.skip), ("sel", s.sel_in, s.sel), ("b", s.b_in, s.b),
        ("c", s.c_in, s.c), ("wb", s.conv_b, s.wb), ("wc", s.conv_c, s.wc), ("x", s.x_in, s.x),
        ("wx", s.conv_x, s.wx), ("z", s.z_in, s.z), ("gain", s.gain_in, s.gain),
        ("value", s.value_in, s.value), ("bk", s.bucket, s.bk), ("tab", s.table, s.tab),
    ]):
        load[name] = loader(src, dst, i)
        load[name]().start()

    def loaded(*which):
        for name in which:
            load[name]().wait()

    barrier = pltpu.get_barrier_semaphore()

    def greet(device):
        pl.semaphore_signal(barrier, inc=1, device_id=device, device_id_type=MESH)

    greet(sib)
    for d in range(1, RING):
        greet({"ctx": chip(d)})
        greet({"ctx": chip(d), "tp": 1 - tp})
    pl.when(upper_level)(lambda: greet({"ctx": ctx + RING}))
    pl.when(lower_level)(lambda: greet({"ctx": ctx - RING}))
    pl.when(cross_next)(lambda: greet(next_block))
    pl.when(cross_prev)(lambda: greet(prev_block))

    def one(flag):
        return jnp.where(flag, 1, 0)

    row_i, col_i = iota((T, T), 0), iota((T, T), 1)
    eye = row_i == col_i
    lower = row_i >= col_i

    def column(row):
        return jnp.sum(jnp.where(eye, row, 0.0), axis=1, keepdims=True)

    loaded("rs")
    real = jnp.broadcast_to(column(s.rs[pl.ds(tp, 1), :].astype(f32)), (T, LANES))
    s.pos[0:8, :] = jnp.zeros((8, LANES), f32)
    s.pos[8 : 8 + T, :] = real
    last_r = s.pos[T + 7 : T + 8, :]
    last_two = jnp.maximum(last_r, s.pos[T + 6 : T + 7, :])
    at = iota((16, LANES), 0)
    keep = jnp.where(at == 13, 1.0 - last_two, jnp.where(at == 14, 1.0 - last_r, 1.0))
    s.keep[...] = keep
    keep8 = keep[8:16, 0:1]

    loaded("xt", "bt", "ct")
    ends = [ref[...].astype(f32)[8:16] * keep8 for ref in (s.xt, s.bt, s.ct)]
    ends = jnp.concatenate(ends, axis=1)
    quarter = (W + 2 * N) // 4
    for q in range(4):
        s.halo_wide[4 * q : 4 * q + 4, :] = ends[4:8, q * quarter : (q + 1) * quarter]
    s.halo_out[...] = s.halo_wide[...].astype(bf16)
    loaded("dt", "rate", "bias", "skip")
    rate, skip = s.rate[...], s.skip[...]
    dtp = s.dt_raw[...].astype(f32).T + s.bias[...]
    dt = jnp.maximum(dtp, 0.0) + jnp.log1p(jnp.exp(-jnp.abs(dtp)))
    s.dtp[...] = dtp
    s.dt[...] = dt
    low = jnp.where(lower, 1.0, 0.0).astype(bf16)
    cum = exact_dot(low, -dt * rate)
    counts = dot(low, real.astype(bf16))
    total = counts[T - 1 : T, :]
    cum_end = cum[T - 1 : T, :]
    eend = jnp.exp(cum_end)
    decay = eend * jnp.where(total[:, :H] == 0.0, 1.0, 0.0)
    s.dec_out[...] = jnp.broadcast_to(twice(decay), (8, 2 * H))

    pl.semaphore_wait(
        barrier,
        2 * RING - 1 + one(upper_level) + one(lower_level) + one(cross_next) + one(cross_prev),
    )
    halo = pltpu.make_async_remote_copy(
        src_ref=s.halo_out, dst_ref=s.halo_in, send_sem=s.halo_sem.at[0],
        recv_sem=s.halo_sem.at[1], device_id=next_block, device_id_type=MESH,
    )
    pl.when(has_next)(lambda: halo.start())

    def tell(d, other):
        return pltpu.make_async_remote_copy(
            src_ref=s.dec_out, dst_ref=s.dec_in.at[2 * me + tp], send_sem=s.dec_sem.at[0],
            recv_sem=s.dec_sem.at[1], device_id={"ctx": chip(d), "tp": lax.rem(tp + other, 2)},
            device_id_type=MESH,
        )

    def all_told():
        ref = s.dec_in.at[0 : 2 * RING - 1]
        return pltpu.make_async_remote_copy(
            src_ref=ref, dst_ref=ref, send_sem=s.dec_sem.at[0], recv_sem=s.dec_sem.at[1],
            device_id=sib, device_id_type=MESH,
        )

    for d in range(RING):
        for other in range(2):
            if d + other > 0:
                tell(d, other).start()
    s.dec_in[2 * me + tp] = s.dec_out[...]

    s.mask[...] = jnp.where(jnp.logical_and(lower, counts == counts.T), 1.0, 0.0)
    s.start_alive[...] = jnp.where(counts == 0.0, 1.0, 0.0)
    s.end_alive[...] = jnp.where(counts == total, 1.0, 0.0)
    one_back, two_back = s.pos[7 : 7 + T, :], s.pos[6 : 6 + T, :]
    second = jnp.maximum(real, one_back)
    for k, flag in enumerate([real, second, jnp.maximum(second, two_back)]):
        s.valid[k] = 1.0 - flag
    for k in range(3):
        m = k + 1
        s.shifted[k, 0:8, :] = jnp.zeros((8, LANES), f32)
        s.shifted[k, T : T + 8, :] = jnp.zeros((8, LANES), f32)
        s.shifted[k, 8 - m : 8 - m + T, :] = s.valid[k]
    for i in range(4):
        s.first_back[i, 0:8, :] = jnp.zeros((8, LANES), f32)
        s.back[i, 0:8, :] = jnp.zeros((8, LANES), f32)
        s.back[i, T + 8 : T + 16, :] = jnp.zeros((8, LANES), f32)
    s.ehl[...] = jnp.concatenate(two(jnp.exp(cum)), axis=1)
    s.whl[...] = jnp.concatenate(two(jnp.exp(-cum) * dt), axis=1)

    def spread(rows, out):
        halves = jnp.concatenate(two(rows), axis=1)
        for j in range(C):
            out[j] = dot(halves, s.sel[j])

    loaded("sel")
    spread(jnp.concatenate([eend, decay, skip] + [jnp.zeros((1, H), f32)] * 5, axis=0), s.rows)
    loaded("b", "c", "wb", "wc", "x", "wx")

    def conv_pre(slot, piece, tail, w):
        ext = s.ext.at[slot]
        ext[0:8, :] = tail
        ext[8 : 8 + T, :] = piece
        u = w[0:1] * piece
        for k in range(1, 4):
            u = u + (w[k : k + 1] * ext[8 - k : 8 - k + T, :]) * s.valid[k - 1]
        return u

    def conv_back(slot, du, w):
        ext = s.back.at[slot]
        ext[8 : 8 + T, :] = du
        g = w[0:1] * ext[0 : T + 8, :]
        for k in range(1, 4):
            g = g + (w[k : k + 1] * ext[k : k + T + 8, :]) * s.shifted[k - 1]
        return g[0:8], g[8:]

    def silu_both(u):
        sg = sigmoid(u)
        value = u * sg
        return value.astype(bf16), sg + value * (1.0 - sg)

    def lanes(j, i):
        return pl.ds(pl.multiple_of(j * WIDE + i * LANES, LANES), LANES)

    def cols(i):
        return slice(i * LANES, (i + 1) * LANES)

    PART = STATE // RING
    OTHERS = RING - 1

    def rows_of(d):
        return pl.ds(pl.multiple_of(member(d) * PART, PART), PART)

    def ship(way, kind, k, src, dst, device):
        return pltpu.make_async_remote_copy(
            src_ref=src, dst_ref=dst, send_sem=s.sent.at[way, kind],
            recv_sem=s.came_sem.at[way, kind, k], device_id=device, device_id_type=MESH,
        )

    def to_sib(way, k):
        return ship(way, 0, k, s.add.at[way, 2 * k + 1 - tp], s.sib_add.at[way, k], sib)

    def to_owner(way, d, k):
        src, dst = s.chip_add.at[way, k, rows_of(d)], s.parts.at[way, me, k]
        return ship(way, 1, k, src, dst, {"ctx": chip(d)})

    def along(way, k):
        device = {"ctx": ctx + (RING if way == 0 else -RING)}
        return ship(way, 2, k, s.going.at[way, k], s.came.at[way, k], device)

    def from_owner(way, d, k):
        src, dst = s.starts.at[way, member(d), k], s.chip_start.at[way, k, rows_of(0)]
        return ship(way, 3, k, src, dst, {"ctx": chip(d)})

    def arrived(way, kind, k):
        ref = (
            s.sib_add.at[way, k],
            s.parts.at[way, 0:OTHERS, k],
            s.came.at[way, k],
            s.chip_start.at[way, k, 0 : OTHERS * PART],
            s.sib_start.at[way, k],
        )[kind]
        ship(way, kind, k, ref, ref, sib).wait_recv()

    def all_sent(way, kind):
        ref = (
            s.sib_add.at[way],
            s.chip_add.at[way, :, 0 : OTHERS * PART],
            s.going.at[way],
            s.starts.at[way, 0:OTHERS],
            s.sib_start.at[way],
        )[kind]
        ship(way, kind, 0, ref, ref, sib).wait_send()

    def start_ref(way, j):
        return (s.xs if way == 0 else s.qg).at[j, T : 2 * T, :]

    def back_to_sib(way, k):
        return ship(
            way, 4, k, s.sib_start.at[way, k], start_ref(way, 2 * k + tp), sib
        )

    def before(way):
        return lower_level if way == 0 else upper_level

    def after(way):
        return upper_level if way == 0 else lower_level

    def merge_chip(way, k):
        arrived(way, 0, k)
        j = 2 * k + tp
        own, other = s.rows[j, 1:2, :], s.peer_rows[j, RING : RING + 1, :]
        first = tp == way
        ca = jnp.where(first, other, 1.0)
        cb = jnp.where(first, 1.0, own)
        a, b = s.add[way, j].astype(f32), s.sib_add[way, k].astype(f32)
        s.chip_add[way, k] = (ca * a + cb * b).astype(bf16)
        for d in range(1, RING):
            to_owner(way, d, k).start()
        s.parts[way, me, k] = s.chip_add[way, k, rows_of(0), :]

    def merge_square(way, k):
        arrived(way, 1, k)
        pl.when(before(way))(lambda: arrived(way, 2, k))
        state = jnp.where(before(way), s.came[way, k].astype(f32), 0.0)
        decay_rows = s.peer_rows[2 * k + tp]
        for m in range(RING) if way == 0 else range(RING - 1, -1, -1):
            s.starts[way, m, k] = state.astype(bf16)
            state = decay_rows[m : m + 1, :] * state + s.parts[way, m, k].astype(f32)
        s.going[way, k] = state.astype(bf16)
        pl.when(after(way))(lambda: along(way, k).start())
        s.chip_start[way, k, rows_of(0), :] = s.starts[way, me, k]

    def give(way, k):
        for d in range(1, RING):
            from_owner(way, d, k).start()

    def split_chip(way, k):
        arrived(way, 3, k)
        j = 2 * k + tp
        own, other = s.rows[j, 1:2, :], s.peer_rows[j, RING : RING + 1, :]
        t_first = tp == way
        start = s.chip_start[way, k]
        ahead = jnp.where(t_first, s.add[way, j], s.sib_add[way, k]).astype(f32)
        later = (jnp.where(t_first, own, other) * start.astype(f32) + ahead).astype(bf16)
        s.sib_start[way, k] = jnp.where(t_first, later, start)
        back_to_sib(way, k).start()
        start_ref(way, j)[...] = jnp.where(t_first, start, later)

    def start_group(g):
        at_g = pl.ds(pl.multiple_of(g * STATE, STATE), STATE)
        at_b = pl.ds(pl.multiple_of(W + g * STATE, STATE), STATE)
        at_c = pl.ds(pl.multiple_of(W + N + g * STATE, STATE), STATE)
        ub = conv_pre(0, s.b[:, at_g].astype(f32), s.tail[:, at_b], s.wb[:, at_g])
        uc = conv_pre(1, s.c[:, at_g].astype(f32), s.tail[:, at_c], s.wc[:, at_g])
        bb, s.ub[g] = silu_both(ub)
        cb, s.uc[g] = silu_both(uc)
        s.bc[g] = bb
        s.cc[g] = cb
        scores = dot(cb, bb, 1, 1) * s.mask[...]
        ba, cr = bb.astype(f32) * s.end_alive[...], cb.astype(f32) * s.start_alive[...]
        s.gcr[g] = jnp.concatenate([scores, cr], axis=1).astype(bf16)
        s.gtb[g] = jnp.concatenate([scores.T, ba], axis=1).astype(bf16)
        s.bat[g] = ba.T.astype(bf16)
        s.crt[g] = cr.T.astype(bf16)

    def conv_first(k, carry=None):
        for jj in range(2):
            j = 2 * k + jj
            weight = dot(s.whl[...], s.sel[j])
            for i in range(2):
                at_x = lanes(j, i)
                none = jnp.zeros((8, LANES), f32)
                u = conv_pre(2 * jj + i, s.x[:, at_x].astype(f32), none, s.wx[:, at_x])
                xc, s.us[j, :, cols(i)] = silu_both(u)
                s.xc[j, :, cols(i)] = xc
                s.xs[j, 0:T, cols(i)] = (xc.astype(f32) * weight[:, cols(i)]).astype(bf16)
        return carry

    def phase_conv(k):
        g = lax.div(k, per)
        pl.when(lax.rem(k, per) == 0)(lambda: start_group(g))
        for jj in range(2):
            j = 2 * k + jj
            weight = dot(s.whl[0:16, :], s.sel[j])
            for i in range(2):
                at_x = lanes(j, i)
                ext = s.first_rows.at[2 * jj + i]
                piece = s.x[0:16, at_x].astype(f32)
                ext[0:8, :] = s.tail[:, at_x]
                ext[8:24, :] = piece
                w = s.wx[:, at_x]
                u = w[0:1] * piece
                for m in range(1, 4):
                    u = u + (w[m : m + 1] * ext[8 - m : 24 - m, :]) * s.valid[m - 1, 0:16, :]
                xc, s.us[j, 0:16, cols(i)] = silu_both(u)
                s.xc[j, 0:16, cols(i)] = xc
                s.xs[j, 0:16, cols(i)] = (xc.astype(f32) * weight[:, cols(i)]).astype(bf16)
            s.add[0, j] = (dot(s.bat[g], s.xs[j, 0:T, :]) * s.rows[j, 0:1, :]).astype(bf16)
        to_sib(0, k).start()

    lax.fori_loop(0, EARLY, conv_first, None)

    @pl.when(has_prev)
    def _():
        halo.wait_recv()

    @pl.when(jnp.logical_not(has_prev))
    def _():
        s.halo_in[...] = jnp.zeros(s.halo_in.shape, bf16)

    s.halo_wide[...] = s.halo_in[...].astype(f32)
    for q in range(4):
        s.tail[4:8, q * quarter : (q + 1) * quarter] = s.halo_wide[4 * q : 4 * q + 4, :]

    def run(steps, total):
        def body(i, carry):
            for start, count, step in steps:
                pl.when(jnp.logical_and(i >= start, i < start + count))(
                    partial(step, i - start)
                )
            return carry

        lax.fori_loop(0, total, body, 0)

    def meet_peers(_):
        all_told().wait_recv()
        got = [s.dec_in[i, 0:1, :H] for i in range(2 * RING)]
        chips = [got[2 * m] * got[2 * m + 1] for m in range(RING)]
        other = s.dec_in[2 * me + 1 - tp, 0:1, :H]
        rest = [jnp.zeros((7 - RING, H), f32)]
        spread(jnp.concatenate(chips + [other] + rest, axis=0), s.peer_rows)

    s.sq[...] = jnp.zeros(s.sq.shape, f32)
    s.nu[...] = jnp.zeros(s.nu.shape, f32)

    def prepare_mix(_):
        loaded("z", "gain", "value", "bk", "tab")
        s.gw[...] = s.gain[...] * s.value[...]
        place = column(s.bk[pl.ds(tp, 1), :].astype(f32))
        tabled = jnp.where(place == iota((T, tn), 1).astype(f32), s.tab[...], 0.0)
        s.target[...] = jnp.broadcast_to(jnp.sum(tabled, axis=1, keepdims=True), (T, LANES))

    def phase_mix(k):
        g = lax.div(k, per)
        arrived(0, 4, k)
        for jj in range(2):
            j = 2 * k + jj
            yr = dot(s.gcr[g], s.xs[j])
            s.yr[j] = yr
            carried = s.rows[j, 1:2, :] * s.xs[j, T : 2 * T, :].astype(f32)
            s.end[j] = (s.add[0, j].astype(f32) + carried).astype(bf16)
            reach = dot(s.ehl[...], s.sel[j])
            for i in range(2):
                at_x = lanes(j, i)
                m = reach[:, cols(i)] * yr[:, cols(i)]
                m = m + s.rows[j, 2:3, cols(i)] * s.xc[j, :, cols(i)].astype(f32)
                z = s.z[:, at_x].astype(f32)
                gated = m * (z * sigmoid(z))
                s.sq[...] += gated * gated
                s.nu[...] += gated * s.gw[:, at_x]

    first = F_LAG + F_WAIT * one(before(0))
    given = first + F_GIVE * one(after(0))
    run(
        [
            (first, K, partial(merge_square, 0)),
            (given, K, partial(give, 0)),
            (given + F_SPLIT, K, partial(split_chip, 0)),
            (0, K, phase_conv),
            (0, K - EARLY, lambda k: conv_first(k + EARLY)),
            (1, 1, meet_peers),
            (1, K, partial(merge_chip, 0)),
            (K, 1, prepare_mix),
            (given + F_MIX, K, phase_mix),
        ],
        F_LAG + F_WAIT + F_GIVE + F_MIX + K,
    )

    squares = jnp.sum(s.sq[...], axis=1, keepdims=True)
    numer = jnp.sum(s.nu[...], axis=1, keepdims=True)
    rms = jnp.sqrt(squares / W + epsilon)
    values = numer / rms
    vscale = (values - s.target[...]) / rms
    s.vs[...] = vscale
    s.co[...] = jnp.broadcast_to(values / (rms * W), (T, LANES))
    s.vals[...] = jnp.sum(jnp.where(eye, values, 0.0), axis=0, keepdims=True)

    stores = []

    def store(src, dst, i):
        copy = pltpu.make_async_copy(src, dst, s.out_sem.at[i])
        copy.start()
        stores.append(copy)

    store(s.vals, s.o_values, 0)

    s.h1[...] = jnp.zeros(s.h1.shape, f32)
    s.h_end[...] = jnp.zeros(s.h_end.shape, f32)
    s.h2[...] = jnp.zeros(s.h2.shape, f32)

    def head_sums(v, j):
        return dot(v.astype(bf16), s.sel[j], 1, 1)

    def phase_back(k):
        g = lax.div(k, per)
        for jj in range(2):
            j = 2 * k + jj
            reach = dot(s.ehl[...], s.sel[j])
            pieces = []
            for i in range(2):
                at_x = lanes(j, i)
                e, yr = reach[:, cols(i)], s.yr[j, :, cols(i)]
                m = e * yr + s.rows[j, 2:3, cols(i)] * s.xc[j, :, cols(i)].astype(f32)
                z = s.z[:, at_x].astype(f32)
                sg = sigmoid(z)
                gate = z * sg
                gated = m * gate
                dg = s.vs[...] * (s.gw[:, at_x] - s.co[...] * gated)
                s.gz[:, at_x] = (dg * m * (sg + gate * (1.0 - sg))).astype(bf16)
                dy = dg * gate
                s.dy[j, :, cols(i)] = dy
                q = (e * dy).astype(bf16)
                s.qg[j, 0:T, cols(i)] = q
                pieces.append(q.astype(f32) * yr)
            s.h2[...] += head_sums(jnp.concatenate(pieces, axis=1), j)
            s.add[1, j] = dot(s.crt[g], s.qg[j, 0:T, :]).astype(bf16)
        to_sib(1, k).start()

    def edge(at):
        return pltpu.make_async_remote_copy(
            src_ref=s.edge_out.at[at], dst_ref=s.edge_in.at[at], send_sem=s.edge_sem.at[0],
            recv_sem=s.edge_sem.at[1], device_id=prev_block, device_id_type=MESH,
        )

    def gx_part(k):
        at_k = pl.ds(pl.multiple_of(k * 2 * WIDE, 2 * WIDE), 2 * WIDE)
        return pltpu.make_async_copy(
            s.gx.at[0 : T - 16, at_k], s.o_gx.at[0 : T - 16, at_k], s.out_sem.at[6]
        )

    def finish(k, i, slot, du, w, out, at_o):
        head_rows, grad = conv_back(slot, du, w)
        s.last[k, :, cols(i)] = grad[T - 16 :, :]
        out[:, at_o] = grad.astype(bf16)
        return head_rows

    def finish_edge(k, i, *rest):
        s.edge_out[k, :, cols(i)] = finish(k, i, *rest)[4:8]

    def phase_scores(g):
        both = jnp.zeros((T, 2 * T), f32)
        for q in range(2 * per):
            j = 2 * per * g + q
            both = both + dot(s.qg[j, 0:T, :], s.xs[j], 1, 1)
        ds = (both[:, :T] * s.mask[...]).astype(bf16)
        dc = dot(ds, s.bc[g]) + both[:, T:] * s.start_alive[...]
        s.dbs[g] = dot(ds, s.cc[g], 0, 0)
        at_g = pl.ds(pl.multiple_of(g * STATE, STATE), STATE)
        finish_edge(per * g + per - 1, 5, 1, dc * s.uc[g], s.wc[:, at_g], s.gc, at_g)

    def phase_edge(k):
        g = lax.div(k, per)
        arrived(1, 4, k)

        @pl.when(lax.rem(k, per) == 0)
        def _():
            s.dbacc[...] = jnp.zeros(s.dbacc.shape, f32)

        db, h_end = 0.0, 0.0
        for jj in range(2):
            j = 2 * k + jj
            gam = s.qg[j, T : 2 * T, :].astype(f32)
            ends = jnp.sum((gam * s.end[j].astype(f32)).reshape(STATE // 16, 16, WIDE), axis=0)
            h_end = h_end + head_sums(ends, j)
            ge = (gam * s.rows[j, 0:1, :]).astype(bf16)
            s.qg[j, T : 2 * T, :] = ge
            db = db + dot(s.xs[j, 0:T, :], ge, 1, 1)
            dxw = dot(s.gtb[g, 0:16, 0:T], s.qg[j, 0:T, :]) + dot(s.gtb[g, 0:16, T:], ge)
            dx = dot(s.whl[0:16, :], s.sel[j]) * dxw + s.rows[j, 2:3, :] * s.dy[j, 0:16, :]
            for i in range(2):
                ext = s.first_back.at[2 * jj + i]
                ext[8:24, :] = dx[:, cols(i)] * s.us[j, 0:16, cols(i)]
                w = s.wx[:, lanes(j, i)]
                rows = 0.0
                for m in range(1, 4):
                    rows = rows + (w[m : m + 1] * ext[m : m + 8, :]) * s.shifted[m - 1, 0:8, :]
                s.edge_out[k, :, cols(2 * jj + i)] = rows[4:8]
        s.h_end[...] += h_end
        s.dbacc[...] += db

        @pl.when(lax.rem(k, per) == per - 1)
        def _():
            grad_b = s.dbs[g] + s.dbacc[...] * s.end_alive[...]
            at_g = pl.ds(pl.multiple_of(g * STATE, STATE), STATE)
            finish_edge(k, 4, 0, grad_b * s.ub[g], s.wb[:, at_g], s.gb, at_g)

        pl.when(has_prev)(lambda: edge(k).start())

    def phase_last(k):
        g = lax.div(k, per)
        h1 = 0.0
        for jj in range(2):
            j = 2 * k + jj
            dxw = dot(s.gtb[g], s.qg[j])
            h1 = h1 + head_sums(s.xs[j, 0:T, :].astype(f32) * dxw, j)
            dx = dot(s.whl[...], s.sel[j]) * dxw + s.rows[j, 2:3, :] * s.dy[j]
            for i in range(2):
                at_x = lanes(j, i)
                du = dx[:, cols(i)] * s.us[j, :, cols(i)]
                finish(k, 2 * jj + i, 2 * jj + i, du, s.wx[:, at_x], s.gx, at_x)
        s.h1[...] += h1
        gx_part(k).start()

    for k in range(K):
        s.edge_out[k, :, 4 * LANES :] = jnp.zeros((4, 2 * LANES), f32)
        s.last[k, :, 4 * LANES :] = jnp.zeros((16, 2 * LANES), f32)

    def gz_copy():
        return pltpu.make_async_copy(s.gz, s.o_gz, s.out_sem.at[1])

    first = B_LAG + B_WAIT * one(before(1))
    given = first + B_GIVE * one(after(1))
    run(
        [
            (first, K, partial(merge_square, 1)),
            (given, K, partial(give, 1)),
            (given + B_SPLIT, K, partial(split_chip, 1)),
            (0, K, phase_back),
            (1, K, partial(merge_chip, 1)),
            (K, 1, lambda _: gz_copy().start()),
            (given + B_OUT - B_SCORES, G, phase_scores),
            (given + B_OUT, K, phase_edge),
            (given + B_OUT + B_EDGE, K, phase_last),
        ],
        B_LAG + B_WAIT + B_GIVE + B_OUT + B_EDGE + K,
    )

    h1 = s.h1[:, :H]
    dcum = s.h2[:, :H] - h1

    at_end = jnp.sum(s.h_end[:, :H], axis=0, keepdims=True)
    upper = jnp.where(row_i <= col_i, 1.0, 0.0).astype(bf16)
    ddt = h1 / s.dt[...] - s.rate[...] * (exact_dot(upper, dcum) + at_end)
    s.gdt[...] = (ddt * sigmoid(s.dtp[...])).T.astype(bf16)
    store(s.gdt, s.o_gdt, 2)

    @pl.when(jnp.logical_not(has_next))
    def _():
        s.edge_in[...] = jnp.zeros(s.edge_in.shape, f32)

    pl.when(has_next)(lambda: edge(slice(0, K)).wait_recv())

    def fix(k, carry):
        s.last[k, 12:16, :] = s.last[k, 12:16, :] + s.edge_in[k] * s.keep[12:16, 0:1]
        fixed = s.last[k].astype(bf16)
        at_k = pl.ds(pl.multiple_of(k * 2 * WIDE, 2 * WIDE), 2 * WIDE)
        s.gx[T - 16 : T, at_k] = fixed[:, : 2 * WIDE]

        @pl.when(lax.rem(k, per) == per - 1)
        def _():
            at_g = pl.ds(pl.multiple_of(lax.div(k, per) * STATE, STATE), STATE)
            s.gb[T - 16 : T, at_g] = fixed[:, 2 * WIDE : 2 * WIDE + LANES]
            s.gc[T - 16 : T, at_g] = fixed[:, 2 * WIDE + LANES :]

        return carry

    lax.fori_loop(0, K, fix, 0)
    store(s.gx.at[T - 16 : T, :], s.o_gx.at[T - 16 : T, :], 3)
    store(s.gb, s.o_gb, 4)
    store(s.gc, s.o_gc, 5)

    for way in range(2):
        for kind in (0, 1, 3, 4):
            all_sent(way, kind)
        pl.when(after(way))(partial(all_sent, way, 2))
    pl.when(has_prev)(lambda: edge(slice(0, K)).wait_send())
    all_told().wait_send()
    pltpu.make_async_copy(
        s.gx.at[0 : T - 16], s.o_gx.at[0 : T - 16], s.out_sem.at[6]
    ).wait()
    pl.when(has_next)(lambda: halo.wait_send())
    gz_copy().wait()
    for copy in stores:
        copy.wait()


def pass_on(*refs):
    ins, outs, held, sems = refs[:6], refs[6:12], refs[12:18], refs[18]
    pieces = []
    for i, (a, o, h) in enumerate(zip(ins, outs, held)):
        parts = 4 if a.shape[0] * a.shape[1] > 128 * 1024 else 1
        rows = a.shape[0] // parts
        for q in range(parts):
            at = slice(q * rows, (q + 1) * rows)
            come = pltpu.make_async_copy(a.at[at], h.at[at], sems.at[0, i, q])
            go = pltpu.make_async_copy(h.at[at], o.at[at], sems.at[1, i, q])
            come.start()
            pieces.append((come, go))
    for come, go in pieces:
        come.wait()
        go.start()
    for come, go in pieces:
        go.wait()


def shards(
    x_in, b_in, c_in, z_in, dt_raw, conv_x, conv_b, conv_c, decay_rate, dt_bias, skip_scale,
    norm_gain, w_value, resets, bucket, return_table,
):
    T, W = x_in.shape
    N, H = b_in.shape[1], dt_raw.shape[1]
    tn = return_table.shape[0]
    tpn = lax.axis_size("tp")
    C = W // WIDE
    head = np.arange(2 * H)[None, :, None] % H
    lane_head = np.arange(WIDE)[None, None, :] // HEAD_DIM
    chunk_head = np.arange(C)[:, None, None] * (WIDE // HEAD_DIM)
    sel = jnp.asarray(head == lane_head + chunk_head, bf16)
    args = (
        x_in, b_in, c_in, z_in, dt_raw.T, conv_x, conv_b, conv_c, decay_rate[None, :],
        dt_bias[None, :], skip_scale[None, :], norm_gain[None, :], w_value[None, :],
        resets.reshape(tpn, T), bucket.reshape(tpn, T), return_table[None, :], sel,
    )
    table = scratch_table(T, W, N, H, tn)
    anywhere = pl.BlockSpec(memory_space=pl.ANY)
    outs = pl.pallas_call(
        partial(kernel, lax.axis_size("ctx"), tn, (T, W, N, H), tuple(table)),
        out_shape=[
            jax.ShapeDtypeStruct((1, T), f32), jax.ShapeDtypeStruct((T, W), bf16),
            jax.ShapeDtypeStruct((T, N), bf16), jax.ShapeDtypeStruct((T, N), bf16),
            jax.ShapeDtypeStruct((T, W), bf16), jax.ShapeDtypeStruct((H, T), bf16),
        ],
        in_specs=[anywhere] * len(args),
        out_specs=[anywhere] * 6,
        scratch_shapes=list(table.values()),
        compiler_params=pltpu.CompilerParams(
            collective_id=0, has_side_effects=True, vmem_limit_bytes=58 * 1024 * 1024
        ),
    )(*args)
    values, gx, gb, gc, gz, gdt = pl.pallas_call(
        pass_on,
        out_shape=[jax.ShapeDtypeStruct(o.shape, o.dtype) for o in outs],
        in_specs=[anywhere] * 6,
        out_specs=[anywhere] * 6,
        scratch_shapes=[pltpu.VMEM(o.shape, o.dtype) for o in outs]
        + [pltpu.SemaphoreType.DMA((2, 6, 4))],
    )(*outs)
    return values.reshape(T), gx, gb, gc, gz, gdt.T


def solution(mesh):
    row = P(("group", "ctx", "tp"), None)
    seq = P(("group", "ctx"))
    return jax.shard_map(
        shards,
        mesh=mesh,
        in_specs=(row,) * 5 + (P(),) * 8 + (seq, seq, P()),
        out_specs=(P(("group", "ctx", "tp")),) + (row,) * 5,
        check_vma=False,
    )
```
